256 devices in a mesh: mode: 4 (over z_hi), rows: 64 (over z_lo, x, y, core).
Axes of the slice: x: 4, y: 4, z: 8 (z_hi: 4, z_lo: 2; z = z_hi * 2 + z_lo), core: 2. Of those that a mesh axis runs over, the one named last changes fastest.
Arguments:
- object_real: float32 [8, 2048, 2048], P('mode', 'rows'), may hold values from -6 to 6
- object_imag: float32 [8, 2048, 2048], P('mode', 'rows'), may hold values from -6 to 6
- pupil_real: float32 [1024, 1024], P('rows'), may hold values from -0.7 to 0.7
- pupil_imag: float32 [1024, 1024], P('rows'), may hold values from -0.7 to 0.7
- measured: float32 [1, 1024, 1024], P(None, 'rows'), may hold values from 1 to 5
- source_mask: int32 [1, 3], replicated, may hold values from 0 to 1, as said below
- offsets: int32 [3, 2], replicated, may hold values from 0 to 1024
Outputs:
- updated_real: float32 [8, 2048, 2048], P('mode', 'rows')
- updated_imag: float32 [8, 2048, 2048], P('mode', 'rows')
The draws below stay inside these ranges and needn't reach their ends.
Inputs may be any that keep to these rules, and one draw needn't show every extreme that they name: `source_mask`: every frame has at least one LED lit and at least one dark.
All inputs are finite; a program needn't handle non-finite values.
Results may differ from the reference program's by a relative error of at most 0.0003.
Values sent between devices are 32-bit elements; how exact they have to be, the bound alone decides.
A program may use at most 128 MiB of HBM per device.

```python
import jax
import jax.numpy as jnp
from jax import lax

K = 2048
N = 1024
LEDS = 3
FRAMES = 1
MODES = 8


def draw_source_mask(key, part):
    key_bits = jax.random.fold_in(key, 11)
    key_lit = jax.random.fold_in(key, 12)
    key_dark = jax.random.fold_in(key, 13)
    bits = jax.random.randint(key_bits, (FRAMES, LEDS), 0, 2)
    lit_pick = jax.random.randint(key_lit, (FRAMES,), 0, LEDS)
    dark_step = jax.random.randint(key_dark, (FRAMES,), 1, LEDS)
    dark_pick = (lit_pick + dark_step) % LEDS
    columns = jnp.arange(LEDS, dtype=jnp.int32)[None, :]
    forced_on = (columns == lit_pick[:, None]).astype(jnp.int32)
    forced_off = (columns == dark_pick[:, None]).astype(jnp.int32)
    return (jnp.maximum(bits, forced_on) * (1 - forced_off)).astype(jnp.int32)


def plant(array, own_key, least, top_value):
    dims = array.shape
    index_at = [jax.random.randint(jax.random.fold_in(own_key, axis), (), 0, dims[axis]) for axis in range(len(dims))]
    array = array.at[tuple(index_at)].set(least)
    longest = dims.index(max(dims))
    index_at[longest] = (index_at[longest] + 1) % dims[longest]
    return array.at[tuple(index_at)].set(top_value)


def level_of(key, dims, cuts, smallest, largest):
    def one(position, shards_of):
        draws = jax.random.uniform(jax.random.fold_in(jax.random.fold_in(key, 6), position), (shards_of,), jnp.float32, smallest / len(cuts), largest / len(cuts))
        return jnp.repeat(jnp.exp(draws), dims[position] // shards_of).reshape((-1,) + (1,) * (len(dims) - position - 1))

    loudness = one(*cuts[0])
    for cut in cuts[1:]:
        loudness = loudness * one(*cut)
    return loudness


def scatter_about(key, extent, scale, limit, pieces=(), kind=jnp.bfloat16):
    drawn = jax.random.normal(key, extent, jnp.float32) * scale
    if len(pieces) > 0:
        drawn = level_of(key, extent, pieces, -0.22, 0.18) * drawn
    return jnp.clip(drawn, min=-limit, max=limit).astype(kind)


def setup_inputs(seed: int = 0) -> dict:
    key_list = jax.random.split(jax.random.key(seed), 8)
    object_real = scatter_about(key_list[0], (MODES, K, K), 1.0, 6.0, ((0, 4), (1, 64)), jnp.float32)
    object_imag = scatter_about(key_list[1], (MODES, K, K), 1.0, 6.0, ((0, 4), (1, 64)), jnp.float32)
    pupil_real = jnp.clip(jax.random.uniform(key_list[2], (N, N), jnp.float32, -0.7, 0.7) * level_of(key_list[2], (N, N), ((0, 64),), -0.4, 0.0), -0.7, 0.7)
    pupil_imag = jnp.clip(jax.random.uniform(key_list[3], (N, N), jnp.float32, -0.7, 0.7) * level_of(key_list[3], (N, N), ((0, 64),), -0.4, 0.0), -0.7, 0.7)
    measured = jnp.clip(1.0 + 4.0 * jax.random.uniform(key_list[4], (FRAMES, N, N), jnp.float32) ** level_of(key_list[4], (FRAMES, N, N), ((1, 64),), -0.2, 0.2), 1.0, 5.0)
    source_mask = draw_source_mask(jax.random.fold_in(key_list[7], 71), 0)
    offsets = plant(jax.random.randint(key_list[6], (LEDS, 2), 0, K - N + 1), jax.random.fold_in(key_list[6], 1), 0, K - N).astype(jnp.int32)
    return dict(object_real=object_real, object_imag=object_imag, pupil_real=pupil_real, pupil_imag=pupil_imag, measured=measured, source_mask=source_mask, offsets=offsets)


FLOOR_TERM = 0.5

def reference(object_real, object_imag, pupil_real, pupil_imag, measured, source_mask, offsets):
    spectrum = object_real + 1j * object_imag
    pupil_full = jnp.transpose(pupil_real + 1j * pupil_imag)
    weights = source_mask.astype(object_real.dtype)
    anchor = jnp.zeros((), jnp.int32)
    for frame_index in range(FRAMES):
        fields = []
        intensity = jnp.zeros((N, N), object_real.dtype)
        for source_index in range(LEDS):
            start_row = offsets[source_index, 0].astype(jnp.int32)
            start_col = offsets[source_index, 1].astype(jnp.int32)
            window = lax.dynamic_slice(spectrum, (anchor, start_row, start_col), (MODES, N, N))
            wave_field = jnp.fft.ifft2(pupil_full * window, axes=(1, 2), norm='ortho')
            fields.append(wave_field)
            powers = lax.optimization_barrier(jnp.sum(jnp.real(wave_field) ** 2 + jnp.imag(wave_field) ** 2, axis=0))
            intensity = intensity + weights[frame_index, source_index] * powers
        ratios = measured[frame_index] / jnp.sqrt(intensity + FLOOR_TERM)
        for source_index in range(LEDS):
            start_row = offsets[source_index, 0].astype(jnp.int32)
            start_col = offsets[source_index, 1].astype(jnp.int32)
            change = jnp.fft.fft2(weights[frame_index, source_index] * fields[source_index] * (ratios - 1.0), axes=(1, 2), norm='ortho')
            window = lax.dynamic_slice(spectrum, (anchor, start_row, start_col), (MODES, N, N))
            spectrum = lax.dynamic_update_slice(spectrum, window + jnp.conj(pupil_full) * change, (anchor, start_row, start_col))
    return (jnp.real(spectrum), jnp.imag(spectrum))
```

```python
import functools
import math

import jax
import jax.numpy as jnp
import numpy as np
from jax import lax
from jax.experimental import pallas as pl
from jax.experimental.pallas import tpu as pltpu
from jax.sharding import PartitionSpec as P

FLOOR_TERM = 0.5
F32 = jnp.float32
BF16 = jnp.bfloat16
MESH = pl.DeviceIdType.MESH


def tables(n):
    n4 = n // 4
    k = np.arange(n4)
    angle = 2.0 * math.pi * (k[:, None] * k[None, :] % n4) / n4
    t = np.concatenate([np.cos(angle), np.sin(angle)], axis=1) / math.sqrt(n)
    t_hi = t.astype(np.float32).astype(BF16)
    t_lo = (t - t_hi.astype(np.float64)).astype(np.float32).astype(BF16)
    j = np.arange(1, 4)
    tw = 2.0 * math.pi * j[:, None] * k[None, :] / n
    sign = np.where(np.arange(128) < 64, -1.0, 1.0)
    tw_c = np.broadcast_to(np.cos(tw)[:, :, None], (3, n4, 128)).astype(np.float32)
    tw_s = (np.sin(tw)[:, :, None] * sign).astype(np.float32)
    return t_hi, t_lo, tw_c, tw_s


def swap(x):
    return pltpu.roll(x, 64, 1)


def lanes(rows):
    return lax.broadcasted_iota(jnp.int32, (rows, 128), 1)


def trade(v):
    lane = lanes(v[0].shape[0])
    high = lane < 64
    a0 = jnp.where(high, v[0], pltpu.roll(v[2], 64, 1))
    a2 = jnp.where(high, pltpu.roll(v[0], 64, 1), v[2])
    a1 = jnp.where(high, v[1], pltpu.roll(v[3], 64, 1))
    a3 = jnp.where(high, pltpu.roll(v[1], 64, 1), v[3])
    even = lane % 64 < 32
    return (
        jnp.where(even, a0, pltpu.roll(a1, 32, 1)),
        jnp.where(even, pltpu.roll(a0, 96, 1), a1),
        jnp.where(even, a2, pltpu.roll(a3, 32, 1)),
        jnp.where(even, pltpu.roll(a2, 96, 1), a3),
    )


def spread(v):
    lane = lanes(v.shape[0])
    even = lane % 64 < 32
    high = lane < 64
    u0 = jnp.where(even, v, pltpu.roll(v, 32, 1))
    u1 = jnp.where(even, pltpu.roll(v, 96, 1), v)
    r0, r1 = swap(u0), swap(u1)
    return (
        jnp.where(high, u0, r0),
        jnp.where(high, u1, r1),
        jnp.where(high, r0, u0),
        jnp.where(high, r1, u1),
    )


def split_bf16(x):
    hi = x.astype(BF16)
    return hi, (x - hi.astype(F32)).astype(BF16)


def put(rhs, n4, block, r, rows, a, sign):
    cols = slice(128 * block, 128 * block + 128)
    turned = swap(a) * jnp.where(lanes(rows) < 64, -sign, sign)
    hi, lo = split_bf16(a)
    t_hi, t_lo = split_bf16(turned)
    rhs[pl.ds(r, rows), cols] = hi
    rhs[pl.ds(n4 + r, rows), cols] = t_hi
    rhs[pl.ds(2 * n4 + r, rows), cols] = lo
    rhs[pl.ds(3 * n4 + r, rows), cols] = t_lo


def product(rhs, t_hi, t_lo, out, n4):
    for half in range(2):
        cols = slice(256 * half, 256 * half + 256)
        dot = functools.partial(jnp.dot, preferred_element_type=F32)
        out[:, cols] = (
            dot(t_hi[...], rhs[0 : 2 * n4, cols])
            + dot(t_hi[...], rhs[2 * n4 : 4 * n4, cols])
            + dot(t_lo[...], rhs[0 : 2 * n4, cols])
        )


def butterfly(a, sign, rows):
    e, o = a[0] + a[2], a[1] + a[3]
    d = a[0] - a[2]
    f = swap(a[1] - a[3]) * jnp.where(lanes(rows) < 64, -sign, sign)
    return (e + o, d + f, e - o, d - f)


def twiddle(z, tw_c, tw_s, block, r, rows, sign):
    if block == 0:
        return z
    c = tw_c[block - 1, pl.ds(r, rows), :]
    s = tw_s[block - 1, pl.ds(r, rows), :]
    return z * c + swap(z) * (s * sign)


def over_rows(n4, step, body):
    @pl.loop(0, n4 // step)
    def _(j):
        body(pl.multiple_of(j * step, step))


STEP = 64


def dif(load, sign, n4, rhs, t_hi, t_lo, tw_c, tw_s, out):
    def body(r):
        a = [load(n, r, STEP) for n in range(4)]
        for k, b in enumerate(butterfly(a, sign, STEP)):
            put(rhs, n4, k, r, STEP, twiddle(b, tw_c, tw_s, k, r, STEP, sign), sign)

    over_rows(n4, STEP, body)
    product(rhs, t_hi, t_lo, out, n4)


def dit(load, store, sign, n4, rhs, t_hi, t_lo, tw_c, tw_s, out):
    def fill(r):
        for n in range(4):
            put(rhs, n4, n, r, STEP, load(n, r, STEP), sign)

    over_rows(n4, STEP, fill)
    product(rhs, t_hi, t_lo, out, n4)

    def body(r):
        a = [
            twiddle(out[pl.ds(r, STEP), 128 * n : 128 * n + 128], tw_c, tw_s, n, r, STEP, sign)
            for n in range(4)
        ]
        for k, b in enumerate(butterfly(a, sign, STEP)):
            store(k, r, STEP, b)

    over_rows(n4, STEP, body)


def kernel(
    n,
    plane,
    groups,
    so_re,
    so_im,
    pup_re,
    pup_im,
    meas,
    mask,
    offs,
    t_hi,
    t_lo,
    tw_c,
    tw_s,
    up_re,
    up_im,
    win_out,
    win_in,
    pup_out,
    pup_in,
    meas_out,
    meas_in,
    meas_own,
    p_re,
    p_im,
    field,
    rhs,
    prod,
    lane_out,
    lane_in,
    psi,
    power,
    sum_in,
    ratio_own,
    ratio_all,
    back_out,
    back_in,
    freq,
    upd,
    upd_out,
    upd_in,
    win_sems,
    upd_sems,
    sems,
):
    n4 = n // 4
    ring = 2 * groups
    chunk = n4 // ring
    tiles = n // 128
    cw = min(256, n)
    chunks = n // cw

    mode = lax.axis_index("mode")
    rank = lax.axis_index("rows")
    slot = rank // plane
    here = rank % plane
    level = 2 * mode + slot
    other = (mode, plane * (1 - slot) + here)

    m0, m1, m2 = mask[0, 0], mask[0, 1], mask[0, 2]
    both01 = (m0 * m1) > 0

    def of_slots(j):
        first = jnp.where(m0 > 0, offs[0, j], jnp.where(m1 > 0, offs[1, j], offs[2, j]))
        second = jnp.where(both01, offs[1, j], offs[2, j])
        return first, second

    row0, row1 = of_slots(0)
    col0, col1 = of_slots(1)
    second_lit = jnp.where(m0 + m1 + m2 > 1, 1.0, 0.0).astype(F32)
    mine = slot == 0
    row_mine = jnp.where(mine, row0, row1)
    row_other = jnp.where(mine, row1, row0)
    col_mine = jnp.where(mine, col0, col1)
    col_other = jnp.where(mine, col1, col0)
    weight = jnp.where(mine, jnp.float32(1.0), second_lit)

    barrier = pltpu.get_barrier_semaphore()

    @pl.loop(1, 2 * plane)
    def _(j):
        pl.semaphore_signal(
            barrier, 1, device_id=(mode, (rank + j) % (2 * plane)), device_id_type=MESH
        )

    for g in range(1, groups):
        for i in range(2):
            pl.semaphore_signal(
                barrier,
                1,
                device_id=((mode + g) % groups, plane * i + here),
                device_id_type=MESH,
            )

    col_iota = lax.broadcasted_iota(jnp.int32, (32, cw), 1)
    row_iota = lax.broadcasted_iota(jnp.int32, (32, cw), 0) + 32 * here
    wrapped = jnp.where(row_iota < row_mine, 1, 0)
    stays = wrapped == slot

    def cut(part, c, edge):
        source = (so_re, so_im)[part // 2]
        left = source[part % 2, :, cw * c : cw * c + cw]
        right = source[part % 2, :, n + cw * c : n + cw * c + cw]
        return jnp.where(col_iota + cw * c < edge, right, left)

    for c in range(chunks):
        for part in range(4):
            win_out[c, 32 * part : 32 * part + 32, :] = cut(part, c, col_other)

    for i, turn in enumerate((row0, row1)):
        turned_re = pltpu.roll(pup_re[...], turn, 1)
        turned_im = pltpu.roll(pup_im[...], turn, 1)
        for t in range(tiles):
            cols = slice(128 * t, 128 * t + 128)
            pieces = trade(
                [turned_re[0:8, cols], turned_im[0:8, cols], turned_re[8:16, cols], turned_im[8:16, cols]]
            )
            for d in range(4):
                pup_out[i, 4 * t + d] = pieces[d]

    for t in range(tiles):
        cols = slice(128 * t, 128 * t + 128)
        low, high = meas[0, 0:8, cols], meas[0, 8:16, cols]
        rows8 = []
        for y in range(4):
            rows8.append(
                jnp.concatenate(
                    [low[y : y + 1], low[y + 4 : y + 5], high[y : y + 1], high[y + 4 : y + 5]] * 2,
                    axis=0,
                )
            )
        pieces = trade(rows8)
        for d in range(4):
            meas_out[4 * t + d] = pieces[d]

    pl.semaphore_wait(barrier, 2 * plane - 1 + 2 * (groups - 1))

    def win_copy(c):
        return pltpu.make_async_remote_copy(
            src_ref=win_out.at[c],
            dst_ref=win_in.at[c],
            send_sem=win_sems.at[0, c],
            recv_sem=win_sems.at[1, c],
            device_id=other,
            device_id_type=MESH,
        )

    @pl.loop(1, 2 * plane)
    def _(j):
        to = (rank + j) % (2 * plane)
        pltpu.make_async_remote_copy(
            src_ref=pup_out.at[to // plane, to % plane],
            dst_ref=pup_in.at[rank],
            send_sem=sems.at[0],
            recv_sem=sems.at[1],
            device_id=(mode, to),
            device_id_type=MESH,
        ).start()

    for c in range(chunks):
        win_copy(c).start()

    band = rank // 8
    gives = band // 2 == mode
    to_slot = band % 2
    own_band = gives & (to_slot == slot)

    @pl.when(gives)
    def _():
        @pl.loop(0, plane)
        def _(j):
            to = (here + j) % plane

            @pl.when(plane * to_slot + to != rank)
            def _():
                pltpu.make_async_remote_copy(
                    src_ref=meas_out.at[to],
                    dst_ref=meas_in.at[rank % 8],
                    send_sem=sems.at[2],
                    recv_sem=sems.at[3],
                    device_id=(mode, plane * to_slot + to),
                    device_id_type=MESH,
                ).start()

    def drain(ref, sem):
        pltpu.make_async_copy(ref, ref, sem).wait()

    pup_in[rank] = pup_out[slot, here]
    drain(pup_in.at[pl.ds(0, 2 * plane - 1)], sems.at[1])

    @pl.loop(0, 2 * plane)
    def _(k):
        a_re, a_im, b_re, b_im = spread(pup_in[k])
        sign = jnp.where(lanes(8) < 64, -1.0, 1.0).astype(F32)
        at = pl.multiple_of(16 * k, 16)
        for base in (0, n):
            p_re[pl.ds(base + at, 8), :] = a_re
            p_im[pl.ds(base + at, 8), :] = a_im * sign
            p_re[pl.ds(base + at + 8, 8), :] = b_re
            p_im[pl.ds(base + at + 8, 8), :] = b_im * sign

    turn_col = n - jnp.clip(col_mine, 0, n)

    for c in range(chunks):
        win_copy(c).wait_recv()
        for s in range(cw // 128):
            cols = slice(128 * s, 128 * s + 128)
            parts = []
            for part in range(4):
                own = cut(part, c, col_mine)[:, cols]
                parts.append(
                    jnp.where(stays[:, cols], own, win_in[c, 32 * part : 32 * part + 32, cols])
                )
            w = jnp.concatenate(parts, axis=0).T
            at = cw * c + 128 * s
            pr = p_re[pl.ds(turn_col + at, 128), :]
            pi = p_im[pl.ds(turn_col + at, 128), :]
            field[at : at + 128, :] = pr * w + pi * swap(w)

    args = (n4, rhs, t_hi, t_lo, tw_c, tw_s, prod)

    def keep_freq(k, r, rows, b):
        freq[pl.ds(pl.multiple_of(n4 * k + r, STEP), rows), :] = b

    dit(
        lambda k, r, rows: field[pl.ds(4 * r + k, rows, stride=4), :], keep_freq, 1.0, *args
    )

    @pl.loop(0, tiles)
    def _(j):
        t = (here // 4 + j) % tiles
        turned = freq[pl.ds(pl.multiple_of(128 * t, 128), 128), :].T
        pieces = trade([turned[32 * g : 32 * g + 32] for g in range(4)])
        for d in range(4):
            to = 4 * t + d
            lane_out[to] = pieces[d]

            @pl.when(to != here)
            def _():
                pltpu.make_async_remote_copy(
                    src_ref=lane_out.at[to],
                    dst_ref=lane_in.at[here],
                    send_sem=sems.at[4],
                    recv_sem=sems.at[5],
                    device_id=(mode, plane * slot + to),
                    device_id_type=MESH,
                ).start()

    lane_in[here] = lane_out[here]
    drain(lane_in.at[pl.ds(0, plane - 1)], sems.at[5])

    per = n4 // 32

    def load_lane(k, r, rows):
        first = per * k + r // 32
        return lane_in[pl.ds(first, rows // 32)].reshape(rows, 128)

    dif(load_lane, 1.0, n4, rhs, t_hi, t_lo, tw_c, tw_s, psi)

    def measure_power(r):
        lane = lanes(STEP)
        packed = None
        for k in range(4):
            z = psi[pl.ds(r, STEP), 128 * k : 128 * k + 128]
            p = z * z
            p = p + swap(p)
            p = p + pltpu.roll(p, 32, 1)
            packed = p if packed is None else jnp.where(lane < 32 * k, packed, p)
        power[pl.ds(r, STEP), :] = packed * weight

    over_rows(n4, STEP, measure_power)

    def at_level(j):
        return (j // 2, plane * (j % 2) + here)

    for j in range(1, ring):
        to = (level + j) % ring
        pltpu.make_async_remote_copy(
            src_ref=power.at[pl.ds(pl.multiple_of(chunk * to, chunk), chunk)],
            dst_ref=sum_in.at[level],
            send_sem=sems.at[6],
            recv_sem=sems.at[7],
            device_id=at_level(to),
            device_id_type=MESH,
        ).start()

    @pl.when(own_band)
    def _():
        meas_in[rank % 8] = meas_out[here]
        drain(meas_in.at[pl.ds(0, 7)], sems.at[3])

    @pl.when(jnp.logical_not(own_band))
    def _():
        drain(meas_in.at[pl.ds(0, 8)], sems.at[3])

    for t in range(8):
        meas_own[4 * t : 4 * t + 4, :] = meas_in[t, 0:4, :]

    sum_in[level] = power[pl.ds(pl.multiple_of(chunk * level, chunk), chunk), :]
    drain(sum_in.at[pl.ds(0, ring - 1)], sems.at[7])
    total = sum_in[0]
    for j in range(1, ring):
        total = total + sum_in[j]
    ratio = meas_own[...] / jnp.sqrt(total + FLOOR_TERM) - 1.0
    ratio_own[...] = ratio
    for j in range(1, ring):
        to = (level + j) % ring
        pltpu.make_async_remote_copy(
            src_ref=ratio_own,
            dst_ref=ratio_all.at[level],
            send_sem=sems.at[8],
            recv_sem=sems.at[9],
            device_id=at_level(to),
            device_id_type=MESH,
        ).start()
    ratio_all[level] = ratio
    drain(ratio_all.at[pl.ds(0, ring - 1)], sems.at[9])

    def scale(r):
        f = ratio_all[pl.ds(r // 32, STEP // 32)].reshape(STEP, 128) * weight
        for k, g in enumerate(spread(f)):
            cols = slice(128 * k, 128 * k + 128)
            psi[pl.ds(r, STEP), cols] = psi[pl.ds(r, STEP), cols] * g

    over_rows(n4, STEP, scale)

    def keep_back(k, r, rows, b):
        back_out[pl.ds(per * k + r // 32, rows // 32)] = b.reshape(rows // 32, 32, 128)

    dit(
        lambda k, r, rows: psi[pl.ds(r, rows), 128 * k : 128 * k + 128],
        keep_back,
        -1.0,
        *args,
    )

    @pl.loop(1, plane)
    def _(j):
        to = (here + j) % plane
        pltpu.make_async_remote_copy(
            src_ref=back_out.at[to],
            dst_ref=back_in.at[here],
            send_sem=sems.at[10],
            recv_sem=sems.at[11],
            device_id=(mode, plane * slot + to),
            device_id_type=MESH,
        ).start()

    back_in[here] = back_out[here]
    drain(back_in.at[pl.ds(0, plane - 1)], sems.at[11])

    @pl.loop(0, tiles)
    def _(t):
        pieces = trade([back_in[4 * t + d] for d in range(4)])
        freq[pl.ds(pl.multiple_of(128 * t, 128), 128), :] = jnp.concatenate(pieces, axis=0).T

    dif(
        lambda k, r, rows: freq[pl.ds(pl.multiple_of(n4 * k + r, STEP), rows), :],
        -1.0,
        *args,
    )
    for k in range(4):
        field[pl.ds(k, n4, stride=4), :] = prod[:, 128 * k : 128 * k + 128]

    def upd_copy(c):
        return pltpu.make_async_remote_copy(
            src_ref=upd_out.at[c],
            dst_ref=upd_in.at[c],
            send_sem=upd_sems.at[0, c],
            recv_sem=upd_sems.at[1, c],
            device_id=other,
            device_id_type=MESH,
        )

    for c in range(chunks):
        for s in range(cw // 128):
            cols = slice(128 * s, 128 * s + 128)
            at = cw * c + 128 * s
            v = field[at : at + 128, :]
            pr = p_re[pl.ds(turn_col + at, 128), :]
            pi = p_im[pl.ds(turn_col + at, 128), :]
            e = (pr * v - pi * swap(v)).T
            upd[c, :, cols] = e
            for part in range(4):
                rows = slice(32 * part, 32 * part + 32)
                upd_out[c, rows, cols] = jnp.where(stays[:, cols], 0.0, e[rows])
        upd_copy(c).start()

    for c in range(chunks):
        upd_copy(c).wait_recv()
        lo_mine = col_iota + cw * c < col_mine
        lo_other = col_iota + cw * c < col_other
        for part in range(4):
            rows = slice(32 * part, 32 * part + 32)
            source, target = (so_re, so_im)[part // 2], (up_re, up_im)[part // 2]
            kept = jnp.where(stays, upd[c, rows, :], 0.0)
            got = upd_in[c, rows, :]
            left = slice(cw * c, cw * c + cw)
            right = slice(n + cw * c, n + cw * c + cw)
            m = part % 2
            target[m, :, left] = (
                source[m, :, left] + jnp.where(lo_mine, 0.0, kept) + jnp.where(lo_other, 0.0, got)
            )
            target[m, :, right] = (
                source[m, :, right] + jnp.where(lo_mine, kept, 0.0) + jnp.where(lo_other, got, 0.0)
            )

    for c in range(chunks):
        win_copy(c).wait_send()
        upd_copy(c).wait_send()
    drain(pup_in.at[pl.ds(0, 2 * plane - 1)], sems.at[0])
    for mine_too in (True, False):

        @pl.when(gives & (own_band if mine_too else jnp.logical_not(own_band)))
        def _():
            drain(meas_out.at[pl.ds(0, plane - 1 if mine_too else plane)], sems.at[2])

    drain(lane_out.at[pl.ds(0, plane - 1)], sems.at[4])
    drain(sum_in.at[pl.ds(0, ring - 1)], sems.at[6])
    drain(ratio_all.at[pl.ds(0, ring - 1)], sems.at[8])
    drain(back_out.at[pl.ds(0, plane - 1)], sems.at[10])


def body(groups, object_real, object_imag, pupil_real, pupil_imag, measured, source_mask, offsets):
    n = pupil_real.shape[1]
    plane = n // 32
    n4 = n // 4
    ring = 2 * groups
    cw = min(256, n)
    chunks = n // cw
    consts = [jnp.asarray(t) for t in tables(n)]
    vmem = pl.BlockSpec(memory_space=pltpu.VMEM)
    smem = pl.BlockSpec(memory_space=pltpu.SMEM)
    wide = pltpu.VMEM((chunks, 128, cw), F32)
    blocks = pltpu.VMEM((plane, 32, 128), F32)
    flat = pltpu.VMEM((n, 128), F32)
    scratch = [
        wide,
        wide,
        pltpu.VMEM((2, plane, 8, 128), F32),
        pltpu.VMEM((2 * plane, 8, 128), F32),
        pltpu.VMEM((plane, 8, 128), F32),
        pltpu.VMEM((8, 8, 128), F32),
        pltpu.VMEM((32, 128), F32),
        pltpu.VMEM((2 * n, 128), F32),
        pltpu.VMEM((2 * n, 128), F32),
        flat,
        pltpu.VMEM((n, 512), BF16),
        pltpu.VMEM((n4, 512), F32),
        blocks,
        blocks,
        pltpu.VMEM((n4, 512), F32),
        pltpu.VMEM((n4, 128), F32),
        pltpu.VMEM((ring, n4 // ring, 128), F32),
        pltpu.VMEM((n4 // ring, 128), F32),
        pltpu.VMEM((ring, n4 // ring, 128), F32),
        blocks,
        blocks,
        flat,
        wide,
        wide,
        wide,
        pltpu.SemaphoreType.DMA((2, chunks)),
        pltpu.SemaphoreType.DMA((2, chunks)),
        pltpu.SemaphoreType.DMA((12,)),
    ]
    return pl.pallas_call(
        functools.partial(kernel, n, plane, groups),
        out_shape=[jax.ShapeDtypeStruct(object_real.shape, F32)] * 2,
        in_specs=[vmem] * 5 + [smem] * 2 + [vmem] * 4,
        out_specs=[vmem] * 2,
        scratch_shapes=scratch,
        compiler_params=pltpu.CompilerParams(collective_id=0, has_side_effects=True),
        name="ptycho",
    )(object_real, object_imag, pupil_real, pupil_imag, measured, source_mask, offsets, *consts)


def solution(mesh):
    in_specs = (
        P("mode", "rows", None),
        P("mode", "rows", None),
        P("rows", None),
        P("rows", None),
        P(None, "rows", None),
        P(),
        P(),
    )
    out_specs = (P("mode", "rows", None), P("mode", "rows", None))
    return jax.shard_map(
        functools.partial(body, mesh.shape["mode"]),
        mesh=mesh,
        in_specs=in_specs,
        out_specs=out_specs,
        check_vma=False,
    )
```

```python
import functools
import math

import jax
import jax.numpy as jnp
import numpy as np
from jax import lax
from jax.experimental import pallas as pl
from jax.experimental.pallas import tpu as pltpu
from jax.sharding import PartitionSpec as P

FLOOR_TERM = 0.5
F32 = jnp.float32
BF16 = jnp.bfloat16
MESH = pl.DeviceIdType.MESH


def tables(n):
    n4 = n // 4
    k = np.arange(n4)
    angle = 2.0 * math.pi * (k[:, None] * k[None, :] % n4) / n4
    t = np.concatenate([np.cos(angle), np.sin(angle)], axis=1) / math.sqrt(n)
    t_hi = t.astype(np.float32).astype(BF16)
    t_lo = (t - t_hi.astype(np.float64)).astype(np.float32).astype(BF16)
    lane = np.arange(128)
    residue = 2 * np.arange(2)[:, None] + (lane[None, :] // 32) % 2
    tw = 2.0 * math.pi * residue[:, None, :] * k[None, :, None] / n
    tw_c = np.cos(tw).astype(np.float32)
    tw_s = (np.sin(tw) * np.where(lane < 64, -1.0, 1.0)).astype(np.float32)
    return t_hi, t_lo, tw_c, tw_s


def lanes(rows):
    return lax.broadcasted_iota(jnp.int32, (rows, 128), 1)


def swap(x):
    return pltpu.roll(x, 64, 1)


def is_even(rows):
    return lanes(rows) % 64 < 32


def is_high(rows):
    return lanes(rows) < 64


def times_i(x, sign):
    return swap(x) * jnp.where(is_high(x.shape[0]), -sign, sign)


def pair(a, b):
    even = is_even(a.shape[0])
    return jnp.where(even, a, pltpu.roll(b, 32, 1)), jnp.where(even, pltpu.roll(a, 96, 1), b)


def halves(a, b):
    high = is_high(a.shape[0])
    return jnp.where(high, a, swap(b)), jnp.where(high, swap(a), b)


def trade(v):
    a0, a2 = halves(v[0], v[2])
    a1, a3 = halves(v[1], v[3])
    return (*pair(a0, a1), *pair(a2, a3))


def spread(v):
    u0, u1 = pair(v, v)
    return (*halves(u0, u0), *halves(u1, u1))


def split_bf16(x):
    hi = x.astype(BF16)
    return hi, (x - hi.astype(F32)).astype(BF16)


def put(rhs, n4, block, r, a, sign):
    rows = a.shape[0]
    cols = slice(128 * block, 128 * block + 128)
    hi, lo = split_bf16(a)
    t_hi, t_lo = split_bf16(times_i(a, sign))
    rhs[pl.ds(r, rows), cols] = hi
    rhs[pl.ds(n4 + r, rows), cols] = t_hi
    rhs[pl.ds(2 * n4 + r, rows), cols] = lo
    rhs[pl.ds(3 * n4 + r, rows), cols] = t_lo


def product(rhs, t_hi, t_lo, out, n4):
    dot = functools.partial(jnp.dot, preferred_element_type=F32)
    got = (
        dot(t_hi[...], rhs[0 : 2 * n4, :])
        + dot(t_hi[...], rhs[2 * n4 : 4 * n4, :])
        + dot(t_lo[...], rhs[0 : 2 * n4, :])
    )
    out[0] = got[:, 0:128]
    out[1] = got[:, 128:256]


def butterfly(a, b, sign):
    s, t = a + b, a - b
    even = is_even(a.shape[0])
    x = jnp.where(even, s, pltpu.roll(t, 32, 1))
    y = jnp.where(even, pltpu.roll(s, 96, 1), times_i(t, sign))
    return x + y, x - y


def over(total, step, body):
    for r in range(0, total, step):
        body(r)


def kernel(
    n,
    plane,
    groups,
    hbm_re,
    hbm_im,
    hbm_pr,
    hbm_pi,
    hbm_meas,
    mask,
    offs,
    hbm_thi,
    hbm_tlo,
    hbm_twc,
    hbm_tws,
    out_re,
    out_im,
    so_re,
    so_im,
    pup_re,
    pup_im,
    meas,
    t_hi,
    t_lo,
    tw_c,
    tw_s,
    up_re,
    up_im,
    win_out,
    win_in,
    pup_out,
    pup_in,
    meas_a,
    meas_b,
    meas_out,
    meas_in,
    meas_own,
    p_re,
    p_im,
    w_re,
    w_im,
    rhs,
    prod,
    lane_out,
    lane_in,
    psi,
    power,
    sum_in,
    ratio_own,
    ratio_all,
    back_out,
    back_in,
    upd,
    upd_out,
    upd_in,
    local_sems,
    out_sems,
    win_sems,
    upd_sems,
    lane_sems,
    back_sems,
    sems,
):
    n4 = n // 4
    ring = 2 * groups
    chunk = n4 // ring
    senders = chunk // 4
    tiles = n4 // 128
    per = n4 // 32

    mode = lax.axis_index("mode")
    rank = lax.axis_index("rows")
    slot = rank // plane
    here = rank % plane
    level = 2 * mode + slot
    cross = (mode + groups - 1 + 2 * slot) % groups
    other = (mode, plane * (1 - slot) + here)

    barrier = pltpu.get_barrier_semaphore()

    def greet(where):
        pl.semaphore_signal(barrier, 1, device_id=where, device_id_type=MESH)

    def at_level(j):
        return (j // 2, plane * (j % 2) + here)

    @pl.loop(1, plane)
    def _(j):
        greet((mode, plane * slot + (here + j) % plane))

    @pl.loop(0, plane)
    def _(j):
        greet((cross, plane * (1 - slot) + j))

    for j in range(1, ring - 1):
        greet(at_level((level + j + slot) % ring))

    loads = [
        pltpu.make_async_copy(a, b, local_sems.at[i])
        for i, (a, b) in enumerate(
            (
                (hbm_re, so_re),
                (hbm_im, so_im),
                (hbm_pr, pup_re),
                (hbm_pi, pup_im),
                (hbm_meas, meas),
                (hbm_thi, t_hi),
                (hbm_tlo, t_lo),
                (hbm_twc, tw_c),
                (hbm_tws, tw_s),
            )
        )
    ]
    for i in (2, 3, 0, 1, 4, 5, 6, 7, 8):
        loads[i].start()

    m0, m1, m2 = mask[0, 0], mask[0, 1], mask[0, 2]
    both01 = (m0 * m1) > 0

    def of_slots(j):
        first = jnp.where(m0 > 0, offs[j, 0], jnp.where(m1 > 0, offs[j, 1], offs[j, 2]))
        second = jnp.where(both01, offs[j, 1], offs[j, 2])
        return first, second

    row0, row1 = of_slots(0)
    col0, col1 = of_slots(1)
    second_lit = jnp.where(m0 + m1 + m2 > 1, 1.0, 0.0).astype(F32)
    mine = slot == 0
    row_mine = jnp.where(mine, row0, row1)
    col_mine = jnp.where(mine, col0, col1)
    col_other = jnp.where(mine, col1, col0)
    weight = jnp.where(mine, jnp.float32(1.0), second_lit)

    loads[2].wait()
    loads[3].wait()
    for i, turn in enumerate((row0, row1)):
        turned_re = pltpu.roll(pup_re[...], turn, 1)
        turned_im = pltpu.roll(pup_im[...], turn, 1)
        for t in range(n // 128):
            cols = slice(128 * t, 128 * t + 128)
            pieces = trade(
                [turned_re[0:8, cols], turned_im[0:8, cols], turned_re[8:16, cols], turned_im[8:16, cols]]
            )
            for d in range(4):
                pup_out[i, 4 * t + d] = pieces[d]

    loads[0].wait()
    loads[1].wait()

    def row_stays(width):
        row = lax.broadcasted_iota(jnp.int32, (32, width), 0) + 32 * here
        return jnp.where(row < row_mine, 1, 0) == slot

    def cut(part, m, at, width, edge):
        source = (so_re, so_im)[part]
        col = lax.broadcasted_iota(jnp.int32, (32, width), 1) + at
        return jnp.where(col < edge, source[m, :, n + at : n + at + width], source[m, :, at : at + width])

    wide = min(256, n)
    for m in range(2):
        for part in range(2):
            for at in range(0, n, wide):
                win_out[m, 32 * part : 32 * part + 32, at : at + wide] = cut(
                    part, m, at, wide, col_other
                )

    pl.semaphore_wait(barrier, 2 * plane - 1 + ring - 2)

    def swap_copy(m, src, dst, pair_sems):
        return pltpu.make_async_remote_copy(
            src_ref=src.at[m],
            dst_ref=dst.at[m],
            send_sem=pair_sems.at[0, m],
            recv_sem=pair_sems.at[1, m],
            device_id=other,
            device_id_type=MESH,
        )

    win_copy = [swap_copy(m, win_out, win_in, win_sems) for m in range(2)]
    upd_copy = [swap_copy(m, upd_out, upd_in, upd_sems) for m in range(2)]

    win_copy[0].start()

    def pup_copy(to_mode, to_slot, to):
        pltpu.make_async_remote_copy(
            src_ref=pup_out.at[to_slot, to],
            dst_ref=pup_in.at[rank],
            send_sem=sems.at[0],
            recv_sem=sems.at[1],
            device_id=(to_mode, plane * to_slot + to),
            device_id_type=MESH,
        ).start()

    @pl.loop(0, plane)
    def _(j):
        pup_copy(cross, 1 - slot, (here + j) % plane)

    @pl.loop(1, plane)
    def _(j):
        pup_copy(mode, slot, (here + j) % plane)

    win_copy[1].start()

    band = rank // senders
    to_slot = band % 2
    to_mode = jnp.where(to_slot == slot, mode, cross)
    gives = band // 2 == to_mode
    own_band = gives & (to_slot == slot)

    loads[4].wait()
    stacked = jnp.concatenate(
        [meas[0, :, 128 * t : 128 * t + 128] for t in range(n // 128)], axis=0
    )
    meas_a[...] = stacked.T
    meas_b[...] = jnp.concatenate(
        [meas_a[pl.ds(k, 32, stride=4), :] for k in range(4)], axis=0
    ).T
    pieces = trade([meas_b[pl.ds(y, per * 4, stride=4), :] for y in range(4)])
    for k in range(4):
        for b in range(per):
            meas_out[per * k + b, 0:4, :] = pieces[k][4 * b : 4 * b + 4]
            meas_out[per * k + b, 4:8, :] = pieces[k][4 * b : 4 * b + 4]

    @pl.when(gives)
    def _():
        @pl.loop(0, plane)
        def _(j):
            to = (here + j) % plane

            @pl.when(jnp.logical_not(own_band) | (to != here))
            def _():
                pltpu.make_async_remote_copy(
                    src_ref=meas_out.at[to],
                    dst_ref=meas_in.at[rank % senders],
                    send_sem=sems.at[2],
                    recv_sem=sems.at[3],
                    device_id=(to_mode, plane * to_slot + to),
                    device_id_type=MESH,
                ).start()

    def drain(ref, sem):
        pltpu.make_async_copy(ref, ref, sem).wait()

    pup_in[rank] = pup_out[slot, here]
    drain(pup_in.at[pl.ds(0, 2 * plane - 1)], sems.at[1])

    sign = jnp.where(is_high(8), -1.0, 1.0).astype(F32)
    for k in range(2 * plane):
        a_re, b_re, a_im, b_im = spread(pup_in[k])
        for base in (16 * k, 16 * k + n):
            p_re[base : base + 8, :] = a_re
            p_im[base : base + 8, :] = a_im * sign
            p_re[base + 8 : base + 16, :] = b_re
            p_im[base + 8 : base + 16, :] = b_im * sign

    turn_col = n - jnp.clip(col_mine, 0, n)
    for source, target in ((p_re, w_re), (p_im, w_im)):
        for hi in range(2):
            for r in range(0, n4, 64):
                first = source[pl.ds(turn_col + 2 * hi * n4 + r, 64), :]
                second = source[pl.ds(turn_col + (2 * hi + 1) * n4 + r, 64), :]
                target[hi, r : r + 64, :] = jnp.where(is_even(64), first, second)

    for i in range(5, 9):
        loads[i].wait()

    def twiddle(z, hi, r, sign):
        rows = z.shape[0]
        return z * tw_c[hi, pl.ds(r, rows), :] + swap(z) * (tw_s[hi, pl.ds(r, rows), :] * sign)

    def dif_fill(m, r, a, b, sign):
        for hi, z in enumerate(butterfly(a, b, sign)):
            put(rhs.at[m], n4, hi, r, twiddle(z, hi, r, sign), sign)

    def block_copy(m, src, dst, pair_sems, to):
        pltpu.make_async_remote_copy(
            src_ref=src.at[m, to],
            dst_ref=dst.at[m, here],
            send_sem=pair_sems.at[0, m],
            recv_sem=pair_sems.at[1, m],
            device_id=(mode, plane * slot + to),
            device_id_type=MESH,
        ).start()

    for m in range(2):
        win_copy[m].wait_recv()
        stays = row_stays(128)
        for t in range(tiles):
            x = []
            for hi in range(2):
                pieces = []
                for part in range(2):
                    for lo in range(2):
                        at = n4 * (2 * hi + lo) + 128 * t
                        own = cut(part, m, at, 128, col_mine)
                        got = win_in[m, 32 * part : 32 * part + 32, at : at + 128]
                        pieces.append(jnp.where(stays, own, got))
                w = jnp.concatenate(pieces, axis=0).T
                rows = slice(128 * t, 128 * t + 128)
                x.append(w_re[hi, rows, :] * w + w_im[hi, rows, :] * swap(w))
            dif_fill(m, 128 * t, x[0], x[1], 1.0)
        product(rhs.at[m], t_hi, t_lo, prod.at[m], n4)

        for j in range(2 * tiles):
            u = (here // 8 + j) % (2 * tiles)
            hi, t = u // tiles, u % tiles
            turned = prod[m, hi, pl.ds(pl.multiple_of(128 * t, 128), 128), :].T
            for lo in range(2):
                pieces = trade(
                    [
                        turned[64 * part + 32 * lo + 16 * qh : 64 * part + 32 * lo + 16 * qh + 16]
                        for part in range(2)
                        for qh in range(2)
                    ]
                )
                for d in range(4):
                    to = per * (2 * hi + lo) + 4 * t + d
                    lane_out[m, to] = pieces[d]

                    @pl.when(to != here)
                    def _():
                        block_copy(m, lane_out, lane_in, lane_sems, to)

    for m in range(2):
        lane_in[m, here] = lane_out[m, here]
        drain(lane_in.at[m, pl.ds(0, plane - 1)], lane_sems.at[1, m])

        def fill(r):
            s = r // 32
            a = jnp.concatenate(pair(lane_in[m, s], lane_in[m, per + s]), axis=0)
            b = jnp.concatenate(pair(lane_in[m, 2 * per + s], lane_in[m, 3 * per + s]), axis=0)
            dif_fill(m, r, a, b, 1.0)

        over(n4, 32, fill)
        product(rhs.at[m], t_hi, t_lo, psi.at[m], n4)

    def measure_power(r):
        both = []
        for hi in range(2):
            z0, z1 = psi[0, hi, pl.ds(r, 64), :], psi[1, hi, pl.ds(r, 64), :]
            p = z0 * z0 + z1 * z1
            both.append(p + swap(p))
        power[pl.ds(r, 64), :] = jnp.where(is_high(64), both[0], both[1]) * weight

    over(n4, 64, measure_power)

    for j in range(1, ring):
        to = (level + j) % ring
        pltpu.make_async_remote_copy(
            src_ref=power.at[pl.ds(pl.multiple_of(chunk * to, chunk), chunk)],
            dst_ref=sum_in.at[level],
            send_sem=sems.at[4],
            recv_sem=sems.at[5],
            device_id=at_level(to),
            device_id_type=MESH,
        ).start()

    @pl.when(own_band)
    def _():
        meas_in[rank % senders] = meas_out[here]
        drain(meas_in.at[pl.ds(0, senders - 1)], sems.at[3])

    @pl.when(jnp.logical_not(own_band))
    def _():
        drain(meas_in.at[pl.ds(0, senders)], sems.at[3])

    for t in range(senders):
        meas_own[4 * t : 4 * t + 4, :] = meas_in[t, 0:4, :]

    sum_in[level] = power[pl.ds(pl.multiple_of(chunk * level, chunk), chunk), :]
    drain(sum_in.at[pl.ds(0, ring - 1)], sems.at[5])
    total = sum_in[0]
    for j in range(1, ring):
        total = total + sum_in[j]
    ratio = meas_own[...] / jnp.sqrt(total + FLOOR_TERM) - 1.0
    ratio_own[...] = ratio
    for j in range(1, ring):
        to = (level + j) % ring
        pltpu.make_async_remote_copy(
            src_ref=ratio_own,
            dst_ref=ratio_all.at[level],
            send_sem=sems.at[6],
            recv_sem=sems.at[7],
            device_id=at_level(to),
            device_id_type=MESH,
        ).start()
    ratio_all[level] = ratio
    drain(ratio_all.at[pl.ds(0, ring - 1)], sems.at[7])

    for m in range(2):

        def fill(r):
            f = ratio_all[r // chunk] * weight
            for hi, g in enumerate(halves(f, f)):
                put(rhs.at[m], n4, hi, r, psi[m, hi, pl.ds(r, chunk), :] * g, -1.0)

        over(n4, chunk, fill)
        product(rhs.at[m], t_hi, t_lo, prod.at[m], n4)

        def emit(r):
            s = r // 32
            z = [twiddle(prod[m, hi, pl.ds(r, 32), :], hi, r, -1.0) for hi in range(2)]
            for hi, b in enumerate(butterfly(z[0], z[1], -1.0)):
                first, second = pair(b[0:16], b[16:32])
                back_out[m, 2 * hi * per + s] = first
                back_out[m, (2 * hi + 1) * per + s] = second

        over(n4, 32, emit)

        @pl.loop(1, plane)
        def _(j):
            block_copy(m, back_out, back_in, back_sems, (here + j) % plane)

    for m in range(2):
        back_in[m, here] = back_out[m, here]
        drain(back_in.at[m, pl.ds(0, plane - 1)], back_sems.at[1, m])
        for hi in range(2):
            for t in range(tiles):
                v = [
                    trade([back_in[m, per * (2 * hi + lo) + 4 * t + d] for d in range(4)])
                    for lo in range(2)
                ]
                rows = [
                    v[lo][2 * part + qh] for part in range(2) for lo in range(2) for qh in range(2)
                ]
                put(rhs.at[m], n4, hi, 128 * t, jnp.concatenate(rows, axis=0).T, -1.0)
        product(rhs.at[m], t_hi, t_lo, prod.at[m], n4)
        stays = row_stays(128)
        for t in range(tiles):
            rows = slice(128 * t, 128 * t + 128)
            z = [twiddle(prod[m, hi, rows, :], hi, 128 * t, -1.0) for hi in range(2)]
            for hi, b in enumerate(butterfly(z[0], z[1], -1.0)):
                e = (w_re[hi, rows, :] * b - w_im[hi, rows, :] * swap(b)).T
                for part in range(2):
                    for lo in range(2):
                        at = n4 * (2 * hi + lo) + 128 * t
                        got = e[64 * part + 32 * lo : 64 * part + 32 * lo + 32]
                        to_rows = slice(32 * part, 32 * part + 32)
                        upd[m, to_rows, at : at + 128] = jnp.where(stays, got, 0.0)
                        upd_out[m, to_rows, at : at + 128] = jnp.where(stays, 0.0, got)
        upd_copy[m].start()

    results = []
    for m in range(2):
        upd_copy[m].wait_recv()
        for part in range(2):
            source, target = (so_re, so_im)[part], (up_re, up_im)[part]
            for at in range(0, n, wide):
                col = lax.broadcasted_iota(jnp.int32, (32, wide), 1) + at
                low_mine, low_other = col < col_mine, col < col_other
                to_rows = slice(32 * part, 32 * part + 32)
                kept = upd[m, to_rows, at : at + wide]
                got = upd_in[m, to_rows, at : at + wide]
                left, right = slice(at, at + wide), slice(n + at, n + at + wide)
                target[m, :, left] = (
                    source[m, :, left]
                    + jnp.where(low_mine, 0.0, kept)
                    + jnp.where(low_other, 0.0, got)
                )
                target[m, :, right] = (
                    source[m, :, right]
                    + jnp.where(low_mine, kept, 0.0)
                    + jnp.where(low_other, got, 0.0)
                )
        for part, (a, b) in enumerate(((up_re, out_re), (up_im, out_im))):
            results.append(pltpu.make_async_copy(a.at[m], b.at[m], out_sems.at[m, part]))
            results[-1].start()

    for m in range(2):
        win_copy[m].wait_send()
        upd_copy[m].wait_send()
        drain(lane_out.at[m, pl.ds(0, plane - 1)], lane_sems.at[0, m])
        drain(back_out.at[m, pl.ds(0, plane - 1)], back_sems.at[0, m])
    drain(pup_in.at[pl.ds(0, 2 * plane - 1)], sems.at[0])
    for mine_too in (True, False):

        @pl.when(gives & (own_band if mine_too else jnp.logical_not(own_band)))
        def _():
            drain(meas_out.at[pl.ds(0, plane - 1 if mine_too else plane)], sems.at[2])

    drain(sum_in.at[pl.ds(0, ring - 1)], sems.at[4])
    drain(ratio_all.at[pl.ds(0, ring - 1)], sems.at[6])
    for r in results:
        r.wait()


def body(groups, object_real, object_imag, pupil_real, pupil_imag, measured, source_mask, offsets):
    n = pupil_real.shape[1]
    plane = n // 32
    n4 = n // 4
    ring = 2 * groups
    consts = [jnp.asarray(t) for t in tables(n)]
    anyw = pl.BlockSpec(memory_space=pl.ANY)
    smem = pl.BlockSpec(memory_space=pltpu.SMEM)
    rows = pltpu.VMEM((2, 64, n), F32)
    blocks = pltpu.VMEM((2, plane, 16, 128), F32)
    quarters = pltpu.VMEM((2, n4, 128), F32)
    fields = pltpu.VMEM((2, 2, n4, 128), F32)
    chunks = pltpu.VMEM((ring, n4 // ring, 128), F32)
    like = lambda a: pltpu.VMEM(a.shape, a.dtype)
    pairs = pltpu.SemaphoreType.DMA((2, 2))
    scratch = [
        *[like(a) for a in (object_real, object_imag, pupil_real, pupil_imag, measured)],
        *[like(a) for a in consts],
        like(object_real),
        like(object_imag),
        rows,
        rows,
        pltpu.VMEM((2, plane, 8, 128), F32),
        pltpu.VMEM((2 * plane, 8, 128), F32),
        pltpu.VMEM((128, n // 8), F32),
        pltpu.VMEM((n // 8, 128), F32),
        pltpu.VMEM((plane, 8, 128), F32),
        pltpu.VMEM((n4 // ring // 4, 8, 128), F32),
        pltpu.VMEM((n4 // ring, 128), F32),
        pltpu.VMEM((2 * n, 128), F32),
        pltpu.VMEM((2 * n, 128), F32),
        quarters,
        quarters,
        pltpu.VMEM((2, n, 256), BF16),
        fields,
        blocks,
        blocks,
        fields,
        pltpu.VMEM((n4, 128), F32),
        chunks,
        pltpu.VMEM((n4 // ring, 128), F32),
        chunks,
        blocks,
        blocks,
        rows,
        rows,
        rows,
        pltpu.SemaphoreType.DMA((9,)),
        pairs,
        pairs,
        pairs,
        pairs,
        pairs,
        pltpu.SemaphoreType.DMA((8,)),
    ]
    return pl.pallas_call(
        functools.partial(kernel, n, plane, groups),
        out_shape=[jax.ShapeDtypeStruct(object_real.shape, F32)] * 2,
        in_specs=[anyw] * 5 + [smem] * 2 + [anyw] * 4,
        out_specs=[anyw] * 2,
        scratch_shapes=scratch,
        compiler_params=pltpu.CompilerParams(collective_id=0, has_side_effects=True),
        name="ptycho",
    )(
        object_real,
        object_imag,
        pupil_real,
        pupil_imag,
        measured,
        source_mask,
        offsets.T,
        *consts,
    )


def solution(mesh):
    in_specs = (
        P("mode", "rows", None),
        P("mode", "rows", None),
        P("rows", None),
        P("rows", None),
        P(None, "rows", None),
        P(),
        P(),
    )
    out_specs = (P("mode", "rows", None), P("mode", "rows", None))
    return jax.shard_map(
        functools.partial(body, mesh.shape["mode"]),
        mesh=mesh,
        in_specs=in_specs,
        out_specs=out_specs,
        check_vma=False,
    )
```

```python
import functools
import math

import jax
import jax.numpy as jnp
import numpy as np
from jax import lax
from jax.experimental import pallas as pl
from jax.experimental.pallas import tpu as pltpu
from jax.sharding import PartitionSpec as P

FLOOR_TERM = 0.5
F32 = jnp.float32
BF16 = jnp.bfloat16
MESH = pl.DeviceIdType.MESH


def tables(n):
    n4 = n // 4
    k = np.arange(n4)
    angle = 2.0 * math.pi * (k[:, None] * k[None, :] % n4) / n4
    t = np.concatenate([np.cos(angle), np.sin(angle)], axis=1) / math.sqrt(n)
    t_hi = t.astype(np.float32).astype(BF16)
    t_lo = (t - t_hi.astype(np.float64)).astype(np.float32).astype(BF16)
    lane = np.arange(128)
    residue = 2 * np.arange(2)[:, None] + (lane[None, :] // 32) % 2
    tw = 2.0 * math.pi * residue[:, None, :] * k[None, :, None] / n
    tw_c = np.cos(tw).astype(np.float32)
    tw_s = (np.sin(tw) * np.where(lane < 64, -1.0, 1.0)).astype(np.float32)
    return t_hi, t_lo, tw_c, tw_s


def lanes(rows):
    return lax.broadcasted_iota(jnp.int32, (rows, 128), 1)


def swap(x):
    return pltpu.roll(x, 64, 1)


def is_even(rows):
    return lanes(rows) % 64 < 32


def is_high(rows):
    return lanes(rows) < 64


def times_i(x, sign):
    return swap(x) * jnp.where(is_high(x.shape[0]), -sign, sign)


def pair(a, b):
    even = is_even(a.shape[0])
    return jnp.where(even, a, pltpu.roll(b, 32, 1)), jnp.where(even, pltpu.roll(a, 96, 1), b)


def halves(a, b):
    high = is_high(a.shape[0])
    return jnp.where(high, a, swap(b)), jnp.where(high, swap(a), b)


def trade(v):
    a0, a2 = halves(v[0], v[2])
    a1, a3 = halves(v[1], v[3])
    return (*pair(a0, a1), *pair(a2, a3))


def spread(v):
    u0, u1 = pair(v, v)
    return (*halves(u0, u0), *halves(u1, u1))


def split_bf16(x):
    hi = x.astype(BF16)
    return hi, (x - hi.astype(F32)).astype(BF16)


def put(rhs, n4, block, r, a, sign):
    rows = a.shape[0]
    cols = slice(128 * block, 128 * block + 128)
    hi, lo = split_bf16(a)
    t_hi, t_lo = split_bf16(times_i(a, sign))
    rhs[pl.ds(r, rows), cols] = hi
    rhs[pl.ds(n4 + r, rows), cols] = t_hi
    rhs[pl.ds(2 * n4 + r, rows), cols] = lo
    rhs[pl.ds(3 * n4 + r, rows), cols] = t_lo


def product(rhs, t_hi, t_lo, out, n4):
    dot = functools.partial(jnp.dot, preferred_element_type=F32)
    got = (
        dot(t_hi[...], rhs[0 : 2 * n4, :])
        + dot(t_hi[...], rhs[2 * n4 : 4 * n4, :])
        + dot(t_lo[...], rhs[0 : 2 * n4, :])
    )
    out[0] = got[:, 0:128]
    out[1] = got[:, 128:256]


def butterfly(a, b, sign):
    s, t = a + b, a - b
    even = is_even(a.shape[0])
    x = jnp.where(even, s, pltpu.roll(t, 32, 1))
    y = jnp.where(even, pltpu.roll(s, 96, 1), times_i(t, sign))
    return x + y, x - y


def over(total, step, body):
    for r in range(0, total, step):
        body(r)


def kernel(
    single,
    n,
    plane,
    groups,
    hbm_re,
    hbm_im,
    hbm_pr,
    hbm_pi,
    hbm_meas,
    hbm_mask,
    hbm_offs,
    hbm_thi,
    hbm_tlo,
    hbm_twc,
    hbm_tws,
    out_re,
    out_im,
    mask,
    offs,
    so_re,
    so_im,
    pup_re,
    pup_im,
    meas,
    t_hi,
    t_lo,
    tw_c,
    tw_s,
    win_out,
    win_in,
    pup_out,
    pup_in,
    meas_a,
    meas_b,
    meas_out,
    meas_in,
    meas_own,
    p_re,
    p_im,
    w_re,
    w_im,
    rhs,
    prod,
    lane_out,
    lane_in,
    psi,
    power,
    sum_in,
    ratio_own,
    ratio_all,
    back_out,
    back_in,
    upd,
    upd_out,
    upd_in,
    local_sems,
    win_sems,
    upd_sems,
    lane_sems,
    back_sems,
    sems,
):
    n4 = n // 4
    ring = 2 * groups
    chunk = n4 // ring
    senders = chunk // 4
    tiles = n4 // 128
    per = n4 // 32
    modes = (0,) if single else (0, 1)

    mode = lax.axis_index("mode")
    rank = lax.axis_index("rows")
    slot = rank // plane
    here = rank % plane
    level = 2 * mode + slot
    cross = (mode + groups - 1 + 2 * slot) % groups
    other = (mode, plane * (1 - slot) + here)

    barrier = pltpu.get_barrier_semaphore()

    def greet(where):
        pl.semaphore_signal(barrier, 1, device_id=where, device_id_type=MESH)

    def at_level(j):
        return (j // 2, plane * (j % 2) + here)

    for j in range(plane):
        greet((cross, plane * (1 - slot) + (here + j) % plane))
    for j in range(1, plane):
        greet((mode, plane * slot + (here + j) % plane))

    for j in range(1, ring - 1):
        greet(at_level((level + j + slot) % ring))

    loads = [
        pltpu.make_async_copy(a, b, local_sems.at[i])
        for i, (a, b) in enumerate(
            (
                (hbm_re, so_re),
                (hbm_im, so_im),
                (hbm_pr, pup_re),
                (hbm_pi, pup_im),
                (hbm_meas, meas),
                (hbm_thi, t_hi),
                (hbm_tlo, t_lo),
                (hbm_twc, tw_c),
                (hbm_tws, tw_s),
                (hbm_mask, mask),
                (hbm_offs, offs),
            )
        )
    ]
    for i in (9, 10, 2, 3, 0, 1, 4, 5, 6, 7, 8):
        loads[i].start()

    loads[9].wait()
    loads[10].wait()
    m0, m1, m2 = mask[0, 0], mask[0, 1], mask[0, 2]
    both01 = (m0 * m1) > 0

    def of_slots(j):
        first = jnp.where(m0 > 0, offs[j, 0], jnp.where(m1 > 0, offs[j, 1], offs[j, 2]))
        second = jnp.where(both01, offs[j, 1], offs[j, 2])
        return first, second

    row0, row1 = of_slots(0)
    col0, col1 = of_slots(1)
    second_lit = jnp.where(m0 + m1 + m2 > 1, 1.0, 0.0).astype(F32)
    mine = slot == 0
    if single:
        row_mine, col_mine, col_other, weight = row0, col0, col0, 1.0
    else:
        row_mine = jnp.where(mine, row0, row1)
        col_mine = jnp.where(mine, col0, col1)
        col_other = jnp.where(mine, col1, col0)
        weight = jnp.where(mine, jnp.float32(1.0), second_lit)

    def own_mode(m):
        return slot if single else m

    def other_mode(m):
        return 1 - slot if single else m

    loads[2].wait()
    loads[3].wait()
    for i, turn in enumerate((row0,) if single else (row0, row1)):
        turned_re = pltpu.roll(pup_re[...], turn, 1)
        turned_im = pltpu.roll(pup_im[...], turn, 1)
        for t in range(n // 128):
            cols = slice(128 * t, 128 * t + 128)
            pieces = trade(
                [turned_re[0:8, cols], turned_im[0:8, cols], turned_re[8:16, cols], turned_im[8:16, cols]]
            )
            for d in range(4):
                pup_out[i, 4 * t + d] = pieces[d]

    loads[0].wait()
    loads[1].wait()

    def row_stays(width):
        row = lax.broadcasted_iota(jnp.int32, (32, width), 0) + 32 * here
        return jnp.where(row < row_mine, 1, 0) == slot

    def cut(part, m, at, width, edge):
        source = (so_re, so_im)[part]
        col = lax.broadcasted_iota(jnp.int32, (32, width), 1) + at
        return jnp.where(col < edge, source[m, :, n + at : n + at + width], source[m, :, at : at + width])

    wide = min(256, n)
    for m in modes:
        for part in range(2):
            for at in range(0, n, wide):
                win_out[m, 32 * part : 32 * part + 32, at : at + wide] = cut(
                    part, other_mode(m), at, wide, col_other
                )

    pl.semaphore_wait(barrier, 2 * plane - 1 + ring - 2)

    def swap_copy(m, src, dst, pair_sems):
        return pltpu.make_async_remote_copy(
            src_ref=src.at[m],
            dst_ref=dst.at[m],
            send_sem=pair_sems.at[0, m],
            recv_sem=pair_sems.at[1, m],
            device_id=other,
            device_id_type=MESH,
        )

    win_copy = [swap_copy(m, win_out, win_in, win_sems) for m in modes]
    upd_copy = [swap_copy(m, upd_out, upd_in, upd_sems) for m in modes]

    win_copy[0].start()

    def pup_copy(to_mode, to_slot, to, i):
        pltpu.make_async_remote_copy(
            src_ref=pup_out.at[0 if single else to_slot, to],
            dst_ref=pup_in.at[rank],
            send_sem=sems.at[0],
            recv_sem=sems.at[i],
            device_id=(to_mode, plane * to_slot + to),
            device_id_type=MESH,
        ).start()

    for j in range(plane):
        pup_copy(cross, 1 - slot, (here + j) % plane, 8)
    for j in range(1, plane):
        pup_copy(mode, slot, (here + j) % plane, 1)

    if not single:
        win_copy[1].start()

    band = rank // senders
    to_slot = band % 2
    to_mode = jnp.where(to_slot == slot, mode, cross)
    gives = band // 2 == to_mode
    own_band = gives & (to_slot == slot)

    loads[4].wait()
    stacked = jnp.concatenate(
        [meas[0, :, 128 * t : 128 * t + 128] for t in range(n // 128)], axis=0
    )
    meas_a[...] = stacked.T
    meas_b[...] = jnp.concatenate(
        [meas_a[pl.ds(k, 32, stride=4), :] for k in range(4)], axis=0
    ).T
    pieces = trade([meas_b[pl.ds(y, per * 4, stride=4), :] for y in range(4)])
    for k in range(4):
        for b in range(per):
            meas_out[per * k + b, 0:4, :] = pieces[k][4 * b : 4 * b + 4]
            meas_out[per * k + b, 4:8, :] = pieces[k][4 * b : 4 * b + 4]

    @pl.when(gives)
    def _():
        @pl.loop(0, plane)
        def _(j):
            to = (here + j) % plane

            @pl.when(jnp.logical_not(own_band) | (to != here))
            def _():
                pltpu.make_async_remote_copy(
                    src_ref=meas_out.at[to],
                    dst_ref=meas_in.at[rank % senders],
                    send_sem=sems.at[2],
                    recv_sem=sems.at[3],
                    device_id=(to_mode, plane * to_slot + to),
                    device_id_type=MESH,
                ).start()

    def drain(ref, sem):
        pltpu.make_async_copy(ref, ref, sem).wait()

    pup_in[rank] = pup_out[0 if single else slot, here]
    sign = jnp.where(is_high(8), -1.0, 1.0).astype(F32)
    for half, (count, i) in enumerate(((plane - 1, 1), (plane, 8))):
        drain(pup_in.at[pl.ds(0, count)], sems.at[i])
        first = plane * (slot if half == 0 else 1 - slot)
        for k in range(plane):
            a_re, b_re, a_im, b_im = spread(pup_in[first + k])
            at = pl.multiple_of(16 * first, 16) + 16 * k
            for base in (at, at + n):
                p_re[pl.ds(base, 8), :] = a_re
                p_im[pl.ds(base, 8), :] = a_im * sign
                p_re[pl.ds(base + 8, 8), :] = b_re
                p_im[pl.ds(base + 8, 8), :] = b_im * sign

    turn_col = n - jnp.clip(col_mine, 0, n)
    for source, target in ((p_re, w_re), (p_im, w_im)):
        for hi in range(2):
            for r in range(0, n4, 64):
                first = source[pl.ds(turn_col + 2 * hi * n4 + r, 64), :]
                second = source[pl.ds(turn_col + (2 * hi + 1) * n4 + r, 64), :]
                target[hi, r : r + 64, :] = jnp.where(is_even(64), first, second)

    for i in range(5, 9):
        loads[i].wait()

    def twiddle(z, hi, r, sign):
        rows = z.shape[0]
        return z * tw_c[hi, pl.ds(r, rows), :] + swap(z) * (tw_s[hi, pl.ds(r, rows), :] * sign)

    def dif_fill(m, r, a, b, sign):
        for hi, z in enumerate(butterfly(a, b, sign)):
            put(rhs.at[m], n4, hi, r, twiddle(z, hi, r, sign), sign)

    def block_copy(m, src, dst, pair_sems, to):
        pltpu.make_async_remote_copy(
            src_ref=src.at[m, to],
            dst_ref=dst.at[m, here],
            send_sem=pair_sems.at[0, m],
            recv_sem=pair_sems.at[1, m],
            device_id=(mode, plane * slot + to),
            device_id_type=MESH,
        ).start()

    for m in modes:
        win_copy[m].wait_recv()
        stays = row_stays(128)
        for t in range(tiles):
            x = []
            for hi in range(2):
                pieces = []
                for part in range(2):
                    for lo in range(2):
                        at = n4 * (2 * hi + lo) + 128 * t
                        own = cut(part, own_mode(m), at, 128, col_mine)
                        got = win_in[m, 32 * part : 32 * part + 32, at : at + 128]
                        pieces.append(jnp.where(stays, own, got))
                w = jnp.concatenate(pieces, axis=0).T
                rows = slice(128 * t, 128 * t + 128)
                x.append(w_re[hi, rows, :] * w + w_im[hi, rows, :] * swap(w))
            dif_fill(m, 128 * t, x[0], x[1], 1.0)
        product(rhs.at[m], t_hi, t_lo, prod.at[m], n4)

        for j in range(2 * tiles):
            u = (here // 8 + j) % (2 * tiles)
            hi, t = u // tiles, u % tiles
            turned = prod[m, hi, pl.ds(pl.multiple_of(128 * t, 128), 128), :].T
            for lo in range(2):
                pieces = trade(
                    [
                        turned[64 * part + 32 * lo + 16 * qh : 64 * part + 32 * lo + 16 * qh + 16]
                        for part in range(2)
                        for qh in range(2)
                    ]
                )
                for d in range(4):
                    to = per * (2 * hi + lo) + 4 * t + d
                    lane_out[m, to] = pieces[d]

                    @pl.when(to != here)
                    def _():
                        block_copy(m, lane_out, lane_in, lane_sems, to)

    for m in modes:
        lane_in[m, here] = lane_out[m, here]
        drain(lane_in.at[m, pl.ds(0, plane - 1)], lane_sems.at[1, m])

        def fill(r):
            s = r // 32
            a = jnp.concatenate(pair(lane_in[m, s], lane_in[m, per + s]), axis=0)
            b = jnp.concatenate(pair(lane_in[m, 2 * per + s], lane_in[m, 3 * per + s]), axis=0)
            dif_fill(m, r, a, b, 1.0)

        over(n4, 32, fill)
        product(rhs.at[m], t_hi, t_lo, psi.at[m], n4)

    def measure_power(r):
        both = []
        for hi in range(2):
            p = jnp.zeros((64, 128), F32)
            for m in modes:
                z = psi[m, hi, pl.ds(r, 64), :]
                p = p + z * z
            both.append(p + swap(p))
        power[pl.ds(r, 64), :] = jnp.where(is_high(64), both[0], both[1]) * weight

    over(n4, 64, measure_power)

    for j in range(1, ring):
        to = (level + j) % ring
        pltpu.make_async_remote_copy(
            src_ref=power.at[pl.ds(pl.multiple_of(chunk * to, chunk), chunk)],
            dst_ref=sum_in.at[level],
            send_sem=sems.at[4],
            recv_sem=sems.at[5],
            device_id=at_level(to),
            device_id_type=MESH,
        ).start()

    @pl.when(own_band)
    def _():
        meas_in[rank % senders] = meas_out[here]
        drain(meas_in.at[pl.ds(0, senders - 1)], sems.at[3])

    @pl.when(jnp.logical_not(own_band))
    def _():
        drain(meas_in.at[pl.ds(0, senders)], sems.at[3])

    for t in range(senders):
        meas_own[4 * t : 4 * t + 4, :] = meas_in[t, 0:4, :]

    sum_in[level] = power[pl.ds(pl.multiple_of(chunk * level, chunk), chunk), :]
    drain(sum_in.at[pl.ds(0, ring - 1)], sems.at[5])
    total = sum_in[0]
    for j in range(1, ring):
        total = total + sum_in[j]
    ratio = meas_own[...] / jnp.sqrt(total + FLOOR_TERM) - 1.0
    ratio_own[...] = ratio
    for j in range(1, ring):
        to = (level + j) % ring
        pltpu.make_async_remote_copy(
            src_ref=ratio_own,
            dst_ref=ratio_all.at[level],
            send_sem=sems.at[6],
            recv_sem=sems.at[7],
            device_id=at_level(to),
            device_id_type=MESH,
        ).start()
    ratio_all[level] = ratio
    drain(ratio_all.at[pl.ds(0, ring - 1)], sems.at[7])

    for m in modes:

        def fill(r):
            f = ratio_all[r // chunk] * weight
            for hi, g in enumerate(halves(f, f)):
                put(rhs.at[m], n4, hi, r, psi[m, hi, pl.ds(r, chunk), :] * g, -1.0)

        over(n4, chunk, fill)
        product(rhs.at[m], t_hi, t_lo, prod.at[m], n4)

        def emit(r):
            s = r // 32
            z = [twiddle(prod[m, hi, pl.ds(r, 32), :], hi, r, -1.0) for hi in range(2)]
            for hi, b in enumerate(butterfly(z[0], z[1], -1.0)):
                first, second = pair(b[0:16], b[16:32])
                back_out[m, 2 * hi * per + s] = first
                back_out[m, (2 * hi + 1) * per + s] = second

        over(n4, 32, emit)

        for j in range(1, plane):
            block_copy(m, back_out, back_in, back_sems, (here + j) % plane)

    for m in modes:
        back_in[m, here] = back_out[m, here]
        drain(back_in.at[m, pl.ds(0, plane - 1)], back_sems.at[1, m])
        for hi in range(2):
            for t in range(tiles):
                v = [
                    trade([back_in[m, per * (2 * hi + lo) + 4 * t + d] for d in range(4)])
                    for lo in range(2)
                ]
                rows = [
                    v[lo][2 * part + qh] for part in range(2) for lo in range(2) for qh in range(2)
                ]
                put(rhs.at[m], n4, hi, 128 * t, jnp.concatenate(rows, axis=0).T, -1.0)
        product(rhs.at[m], t_hi, t_lo, prod.at[m], n4)
        stays = row_stays(128)
        for t in range(tiles):
            rows = slice(128 * t, 128 * t + 128)
            z = [twiddle(prod[m, hi, rows, :], hi, 128 * t, -1.0) for hi in range(2)]
            for hi, b in enumerate(butterfly(z[0], z[1], -1.0)):
                e = (w_re[hi, rows, :] * b - w_im[hi, rows, :] * swap(b)).T
                for part in range(2):
                    for lo in range(2):
                        at = n4 * (2 * hi + lo) + 128 * t
                        got = e[64 * part + 32 * lo : 64 * part + 32 * lo + 32]
                        to_rows = slice(32 * part, 32 * part + 32)
                        upd[m, to_rows, at : at + 128] = jnp.where(stays, got, 0.0)
                        upd_out[m, to_rows, at : at + 128] = jnp.where(stays, 0.0, got)
        upd_copy[m].start()

    def finish(m, to_mode, with_kept, with_got):
        for part in range(2):
            source, target = (so_re, so_im)[part], (out_re, out_im)[part]
            to_rows = slice(32 * part, 32 * part + 32)
            for at in range(0, n, wide):
                col = lax.broadcasted_iota(jnp.int32, (32, wide), 1) + at
                left, right = slice(at, at + wide), slice(n + at, n + at + wide)
                low, high = source[to_mode, :, left], source[to_mode, :, right]
                for use, values, edge in (
                    (with_kept, upd, col_mine),
                    (with_got, upd_in, col_other),
                ):
                    if use:
                        v = values[m, to_rows, at : at + wide]
                        low = low + jnp.where(col < edge, 0.0, v)
                        high = high + jnp.where(col < edge, v, 0.0)
                target[to_mode, :, left] = low
                target[to_mode, :, right] = high

    if single:
        finish(0, slot, True, False)
        upd_copy[0].wait_recv()
        finish(0, 1 - slot, False, True)
    else:
        for m in modes:
            upd_copy[m].wait_recv()
            finish(m, m, True, True)

    for m in modes:
        win_copy[m].wait_send()
        upd_copy[m].wait_send()
        drain(lane_out.at[m, pl.ds(0, plane - 1)], lane_sems.at[0, m])
        drain(back_out.at[m, pl.ds(0, plane - 1)], back_sems.at[0, m])
    drain(pup_in.at[pl.ds(0, 2 * plane - 1)], sems.at[0])
    for mine_too in (True, False):

        @pl.when(gives & (own_band if mine_too else jnp.logical_not(own_band)))
        def _():
            drain(meas_out.at[pl.ds(0, plane - 1 if mine_too else plane)], sems.at[2])

    drain(sum_in.at[pl.ds(0, ring - 1)], sems.at[4])
    drain(ratio_all.at[pl.ds(0, ring - 1)], sems.at[6])


def body(groups, object_real, object_imag, pupil_real, pupil_imag, measured, source_mask, offsets):
    n = pupil_real.shape[1]
    plane = n // 32
    n4 = n // 4
    ring = 2 * groups
    consts = [jnp.asarray(t) for t in tables(n)]
    anyw = pl.BlockSpec(memory_space=pltpu.HBM)
    rows = pltpu.VMEM((2, 64, n), F32)
    blocks = pltpu.VMEM((2, plane, 16, 128), F32)
    quarters = pltpu.VMEM((2, n4, 128), F32)
    fields = pltpu.VMEM((2, 2, n4, 128), F32)
    chunks = pltpu.VMEM((ring, n4 // ring, 128), F32)
    like = lambda a: pltpu.VMEM(a.shape, a.dtype)
    pairs = pltpu.SemaphoreType.DMA((2, 2))
    scratch = [
        pltpu.SMEM(source_mask.shape, jnp.int32),
        pltpu.SMEM(offsets.T.shape, jnp.int32),
        *[like(a) for a in (object_real, object_imag, pupil_real, pupil_imag, measured)],
        *[like(a) for a in consts],
        rows,
        rows,
        pltpu.VMEM((2, plane, 8, 128), F32),
        pltpu.VMEM((2 * plane, 8, 128), F32),
        pltpu.VMEM((128, n // 8), F32),
        pltpu.VMEM((n // 8, 128), F32),
        pltpu.VMEM((plane, 8, 128), F32),
        pltpu.VMEM((n4 // ring // 4, 8, 128), F32),
        pltpu.VMEM((n4 // ring, 128), F32),
        pltpu.VMEM((2 * n, 128), F32),
        pltpu.VMEM((2 * n, 128), F32),
        quarters,
        quarters,
        pltpu.VMEM((2, n, 256), BF16),
        fields,
        blocks,
        blocks,
        fields,
        pltpu.VMEM((n4, 128), F32),
        chunks,
        pltpu.VMEM((n4 // ring, 128), F32),
        chunks,
        blocks,
        blocks,
        rows,
        rows,
        rows,
        pltpu.SemaphoreType.DMA((11,)),
        pairs,
        pairs,
        pairs,
        pairs,
        pltpu.SemaphoreType.DMA((9,)),
    ]
    def step(single):
        return pl.pallas_call(
            functools.partial(kernel, single, n, plane, groups),
            out_shape=[pltpu.VMEM(object_real.shape, F32)] * 2,
            in_specs=[anyw] * 11,
            out_specs=[pl.BlockSpec(memory_space=pltpu.VMEM)] * 2,
            scratch_shapes=scratch,
            compiler_params=pltpu.CompilerParams(
                collective_id=1 if single else 0, has_side_effects=True
            ),
            name="one_lit" if single else "two_lit",
        )

    operands = (
        object_real,
        object_imag,
        pupil_real,
        pupil_imag,
        measured,
        source_mask,
        offsets.T,
        *consts,
    )
    return lax.cond(jnp.sum(source_mask) > 1, step(False), step(True), *operands)


def solution(mesh):
    in_specs = (
        P("mode", "rows", None),
        P("mode", "rows", None),
        P("rows", None),
        P("rows", None),
        P(None, "rows", None),
        P(),
        P(),
    )
    out_specs = (P("mode", "rows", None), P("mode", "rows", None))
    return jax.shard_map(
        functools.partial(body, mesh.shape["mode"]),
        mesh=mesh,
        in_specs=in_specs,
        out_specs=out_specs,
        check_vma=False,
    )
```

```python
import functools
import math

import jax
import jax.numpy as jnp
import numpy as np
from jax import lax
from jax.experimental import pallas as pl
from jax.experimental.pallas import tpu as pltpu
from jax.sharding import PartitionSpec as P

FLOOR_TERM = 0.5
F32 = jnp.float32
BF16 = jnp.bfloat16
MESH = pl.DeviceIdType.MESH


def tables(n):
    n4 = n // 4
    k = np.arange(n4)
    angle = 2.0 * math.pi * (k[:, None] * k[None, :] % n4) / n4
    t = np.concatenate([np.cos(angle), np.sin(angle)], axis=1) / math.sqrt(n)
    t_hi = t.astype(np.float32).astype(BF16)
    t_lo = (t - t_hi.astype(np.float64)).astype(np.float32).astype(BF16)
    lane = np.arange(128)
    residue = 2 * np.arange(2)[:, None] + (lane[None, :] // 32) % 2
    tw = 2.0 * math.pi * residue[:, None, :] * k[None, :, None] / n
    tw_c = np.cos(tw).astype(np.float32)
    tw_s = (np.sin(tw) * np.where(lane < 64, -1.0, 1.0)).astype(np.float32)
    return t_hi, t_lo, tw_c, tw_s


def lanes(rows):
    return lax.broadcasted_iota(jnp.int32, (rows, 128), 1)


def swap(x):
    return pltpu.roll(x, 64, 1)


def is_even(rows):
    return lanes(rows) % 64 < 32


def is_high(rows):
    return lanes(rows) < 64


def times_i(x, sign):
    return swap(x) * jnp.where(is_high(x.shape[0]), -sign, sign)


def pair(a, b):
    even = is_even(a.shape[0])
    return jnp.where(even, a, pltpu.roll(b, 32, 1)), jnp.where(even, pltpu.roll(a, 96, 1), b)


def halves(a, b):
    high = is_high(a.shape[0])
    return jnp.where(high, a, swap(b)), jnp.where(high, swap(a), b)


def trade(v):
    a0, a2 = halves(v[0], v[2])
    a1, a3 = halves(v[1], v[3])
    return (*pair(a0, a1), *pair(a2, a3))


def spread(v):
    u0, u1 = pair(v, v)
    return (*halves(u0, u0), *halves(u1, u1))


def split_bf16(x):
    hi = x.astype(BF16)
    return hi, (x - hi.astype(F32)).astype(BF16)


def put(rhs, n4, block, r, a, sign):
    rows = a.shape[0]
    cols = slice(128 * block, 128 * block + 128)
    hi, lo = split_bf16(a)
    t_hi, t_lo = split_bf16(times_i(a, sign))
    rhs[pl.ds(r, rows), cols] = hi
    rhs[pl.ds(n4 + r, rows), cols] = t_hi
    rhs[pl.ds(2 * n4 + r, rows), cols] = lo
    rhs[pl.ds(3 * n4 + r, rows), cols] = t_lo


def product(rhs, t_hi, t_lo, out, n4):
    dot = functools.partial(jnp.dot, preferred_element_type=F32)
    got = (
        dot(t_hi[...], rhs[0 : 2 * n4, :])
        + dot(t_hi[...], rhs[2 * n4 : 4 * n4, :])
        + dot(t_lo[...], rhs[0 : 2 * n4, :])
    )
    out[0] = got[:, 0:128]
    out[1] = got[:, 128:256]


def butterfly(a, b, sign):
    s, t = a + b, a - b
    even = is_even(a.shape[0])
    x = jnp.where(even, s, pltpu.roll(t, 32, 1))
    y = jnp.where(even, pltpu.roll(s, 96, 1), times_i(t, sign))
    return x + y, x - y


def over(total, step, body):
    for r in range(0, total, step):
        body(r)


def kernel(
    single,
    n,
    plane,
    groups,
    hbm_re,
    hbm_im,
    hbm_pr,
    hbm_pi,
    hbm_meas,
    hbm_mask,
    hbm_offs,
    hbm_thi,
    hbm_tlo,
    hbm_twc,
    hbm_tws,
    out_re,
    out_im,
    mask,
    offs,
    so_re,
    so_im,
    pup_re,
    pup_im,
    meas,
    t_hi,
    t_lo,
    tw_c,
    tw_s,
    win_out,
    win_in,
    pup_out,
    pup_in,
    meas_a,
    meas_b,
    meas_out,
    meas_in,
    meas_own,
    p_re,
    p_im,
    w_re,
    w_im,
    rhs,
    prod,
    lane_out,
    lane_in,
    psi,
    power,
    sum_in,
    ratio_own,
    ratio_all,
    back_out,
    back_in,
    upd,
    upd_out,
    upd_in,
    local_sems,
    win_sems,
    upd_sems,
    lane_sems,
    back_sems,
    sems,
):
    n4 = n // 4
    ring = 2 * groups
    chunk = n4 // ring
    senders = chunk // 4
    tiles = n4 // 128
    per = n4 // 32
    modes = (0,) if single else (0, 1)

    mode = lax.axis_index("mode")
    rank = lax.axis_index("rows")
    slot = rank // plane
    here = rank % plane
    level = 2 * mode + slot
    cross = (mode + groups - 1 + 2 * slot) % groups
    other = (mode, plane * (1 - slot) + here)

    wide_x = plane // 8
    across, down, core = here // 8, here // 2 % 4, here % 2
    steps = [(a, b, c) for a in range(wide_x) for b in range(4) for c in range(2)]
    steps.sort(key=lambda s: -min(s[0], wide_x - s[0]) - min(s[1], 4 - s[1]))
    ordered = [
        (s, 8 * ((across + s[0]) % wide_x) + 2 * ((down + s[1]) % 4) + (core + s[2]) % 2)
        for s in steps
    ]
    places = [to for _, to in ordered]
    others = [to for s, to in ordered if s != (0, 0, 0)]

    barrier = pltpu.get_barrier_semaphore()

    def greet(where):
        pl.semaphore_signal(barrier, 1, device_id=where, device_id_type=MESH)

    def at_level(j):
        return (j // 2, plane * (j % 2) + here)

    for to in places:
        greet((cross, plane * (1 - slot) + to))
    for to in others:
        greet((mode, plane * slot + to))

    for j in range(1, ring - 1):
        greet(at_level((level + j + slot) % ring))

    loads = [
        pltpu.make_async_copy(a, b, local_sems.at[i])
        for i, (a, b) in enumerate(
            (
                (hbm_re, so_re),
                (hbm_im, so_im),
                (hbm_pr, pup_re),
                (hbm_pi, pup_im),
                (hbm_meas, meas),
                (hbm_thi, t_hi),
                (hbm_tlo, t_lo),
                (hbm_twc, tw_c),
                (hbm_tws, tw_s),
                (hbm_mask, mask),
                (hbm_offs, offs),
            )
        )
    ]
    for i in (9, 10, 2, 3, 0, 1, 4, 5, 6, 7, 8):
        loads[i].start()

    loads[9].wait()
    loads[10].wait()
    m0, m1, m2 = mask[0, 0], mask[0, 1], mask[0, 2]
    both01 = (m0 * m1) > 0

    def of_slots(j):
        first = jnp.where(m0 > 0, offs[j, 0], jnp.where(m1 > 0, offs[j, 1], offs[j, 2]))
        second = jnp.where(both01, offs[j, 1], offs[j, 2])
        return first, second

    row0, row1 = of_slots(0)
    col0, col1 = of_slots(1)
    second_lit = jnp.where(m0 + m1 + m2 > 1, 1.0, 0.0).astype(F32)
    mine = slot == 0
    if single:
        row_mine, col_mine, col_other, weight = row0, col0, col0, 1.0
    else:
        row_mine = jnp.where(mine, row0, row1)
        col_mine = jnp.where(mine, col0, col1)
        col_other = jnp.where(mine, col1, col0)
        weight = jnp.where(mine, jnp.float32(1.0), second_lit)

    def own_mode(m):
        return slot if single else m

    def other_mode(m):
        return 1 - slot if single else m

    loads[2].wait()
    loads[3].wait()
    for i, turn in enumerate((row0,) if single else (row0, row1)):
        turned_re = pltpu.roll(pup_re[...], turn, 1)
        turned_im = pltpu.roll(pup_im[...], turn, 1)
        for t in range(n // 128):
            cols = slice(128 * t, 128 * t + 128)
            pieces = trade(
                [turned_re[0:8, cols], turned_im[0:8, cols], turned_re[8:16, cols], turned_im[8:16, cols]]
            )
            for d in range(4):
                pup_out[i, 4 * t + d] = pieces[d]

    loads[0].wait()
    loads[1].wait()

    def row_stays(width):
        row = lax.broadcasted_iota(jnp.int32, (32, width), 0) + 32 * here
        return jnp.where(row < row_mine, 1, 0) == slot

    def cut(part, m, at, width, edge):
        source = (so_re, so_im)[part]
        col = lax.broadcasted_iota(jnp.int32, (32, width), 1) + at
        return jnp.where(col < edge, source[m, :, n + at : n + at + width], source[m, :, at : at + width])

    for m in modes:
        for t in range(tiles):
            for q in range(4):
                for part in range(2):
                    win_out[m, t, 32 * part : 32 * part + 32, 128 * q : 128 * q + 128] = cut(
                        part, other_mode(m), n4 * q + 128 * t, 128, col_other
                    )

    pl.semaphore_wait(barrier, 2 * plane - 1 + ring - 2)

    def swap_copy(m, t, src, dst, pair_sems):
        return pltpu.make_async_remote_copy(
            src_ref=src.at[m, t],
            dst_ref=dst.at[m, t],
            send_sem=pair_sems.at[0, m * tiles + t],
            recv_sem=pair_sems.at[1, m * tiles + t],
            device_id=other,
            device_id_type=MESH,
        )

    win_copy = [[swap_copy(m, t, win_out, win_in, win_sems) for t in range(tiles)] for m in modes]
    upd_copy = [[swap_copy(m, t, upd_out, upd_in, upd_sems) for t in range(tiles)] for m in modes]

    for copy in win_copy[0]:
        copy.start()

    def pup_copy(to_mode, to_slot, to, i):
        pltpu.make_async_remote_copy(
            src_ref=pup_out.at[0 if single else to_slot, to],
            dst_ref=pup_in.at[rank],
            send_sem=sems.at[0],
            recv_sem=sems.at[i],
            device_id=(to_mode, plane * to_slot + to),
            device_id_type=MESH,
        ).start()

    for to in places:
        pup_copy(cross, 1 - slot, to, 8)
    for to in others:
        pup_copy(mode, slot, to, 1)

    if not single:
        for copy in win_copy[1]:
            copy.start()

    band = rank // senders
    to_slot = band % 2
    to_mode = jnp.where(to_slot == slot, mode, cross)
    gives = band // 2 == to_mode
    own_band = gives & (to_slot == slot)

    loads[4].wait()
    stacked = jnp.concatenate(
        [meas[0, :, 128 * t : 128 * t + 128] for t in range(n // 128)], axis=0
    )
    meas_a[...] = stacked.T
    meas_b[...] = jnp.concatenate(
        [meas_a[pl.ds(k, 32, stride=4), :] for k in range(4)], axis=0
    ).T
    pieces = trade([meas_b[pl.ds(y, per * 4, stride=4), :] for y in range(4)])
    for k in range(4):
        for b in range(per):
            meas_out[per * k + b, 0:4, :] = pieces[k][4 * b : 4 * b + 4]
            meas_out[per * k + b, 4:8, :] = pieces[k][4 * b : 4 * b + 4]

    @pl.when(gives)
    def _():
        @pl.loop(0, plane)
        def _(j):
            to = (here + j) % plane

            @pl.when(jnp.logical_not(own_band) | (to != here))
            def _():
                pltpu.make_async_remote_copy(
                    src_ref=meas_out.at[to],
                    dst_ref=meas_in.at[rank % senders],
                    send_sem=sems.at[2],
                    recv_sem=sems.at[3],
                    device_id=(to_mode, plane * to_slot + to),
                    device_id_type=MESH,
                ).start()

    def drain(ref, sem):
        pltpu.make_async_copy(ref, ref, sem).wait()

    pup_in[rank] = pup_out[0 if single else slot, here]
    sign = jnp.where(is_high(8), -1.0, 1.0).astype(F32)
    for half, (count, i) in enumerate(((plane - 1, 1), (plane, 8))):
        drain(pup_in.at[pl.ds(0, count)], sems.at[i])
        first = plane * (slot if half == 0 else 1 - slot)
        for k in range(plane):
            a_re, b_re, a_im, b_im = spread(pup_in[first + k])
            at = pl.multiple_of(16 * first, 16) + 16 * k
            for base in (at, at + n):
                p_re[pl.ds(base, 8), :] = a_re
                p_im[pl.ds(base, 8), :] = a_im * sign
                p_re[pl.ds(base + 8, 8), :] = b_re
                p_im[pl.ds(base + 8, 8), :] = b_im * sign

    turn_col = n - jnp.clip(col_mine, 0, n)
    for source, target in ((p_re, w_re), (p_im, w_im)):
        for hi in range(2):
            for r in range(0, n4, 64):
                first = source[pl.ds(turn_col + 2 * hi * n4 + r, 64), :]
                second = source[pl.ds(turn_col + (2 * hi + 1) * n4 + r, 64), :]
                target[hi, r : r + 64, :] = jnp.where(is_even(64), first, second)

    for i in range(5, 9):
        loads[i].wait()

    def twiddle(z, hi, r, sign):
        rows = z.shape[0]
        return z * tw_c[hi, pl.ds(r, rows), :] + swap(z) * (tw_s[hi, pl.ds(r, rows), :] * sign)

    def dif_fill(m, r, a, b, sign):
        for hi, z in enumerate(butterfly(a, b, sign)):
            put(rhs.at[m], n4, hi, r, twiddle(z, hi, r, sign), sign)

    def block_copy(m, src, dst, pair_sems, to):
        pltpu.make_async_remote_copy(
            src_ref=src.at[m, to],
            dst_ref=dst.at[m, here],
            send_sem=pair_sems.at[0, m],
            recv_sem=pair_sems.at[1, m],
            device_id=(mode, plane * slot + to),
            device_id_type=MESH,
        ).start()

    for m in modes:
        stays = row_stays(128)
        for t in range(tiles):
            win_copy[m][t].wait_recv()
            x = []
            for hi in range(2):
                pieces = []
                for part in range(2):
                    for lo in range(2):
                        at = n4 * (2 * hi + lo) + 128 * t
                        own = cut(part, own_mode(m), at, 128, col_mine)
                        q = 128 * (2 * hi + lo)
                        got = win_in[m, t, 32 * part : 32 * part + 32, q : q + 128]
                        pieces.append(jnp.where(stays, own, got))
                w = jnp.concatenate(pieces, axis=0).T
                rows = slice(128 * t, 128 * t + 128)
                x.append(w_re[hi, rows, :] * w + w_im[hi, rows, :] * swap(w))
            dif_fill(m, 128 * t, x[0], x[1], 1.0)
        product(rhs.at[m], t_hi, t_lo, prod.at[m], n4)

        for j in range(2 * tiles):
            hi = (1 + 2 * across // wide_x + j // tiles) % 2
            t = (1 + down // 2 + j) % tiles
            turned = prod[m, hi, pl.ds(pl.multiple_of(128 * t, 128), 128), :].T
            for lo in range(2):
                pieces = trade(
                    [
                        turned[64 * part + 32 * lo + 16 * qh : 64 * part + 32 * lo + 16 * qh + 16]
                        for part in range(2)
                        for qh in range(2)
                    ]
                )
                for d in range(4):
                    to = per * (2 * hi + lo) + 4 * t + d
                    lane_out[m, to] = pieces[d]

                    @pl.when(to != here)
                    def _():
                        block_copy(m, lane_out, lane_in, lane_sems, to)

    for m in modes:
        lane_in[m, here] = lane_out[m, here]
        drain(lane_in.at[m, pl.ds(0, plane - 1)], lane_sems.at[1, m])

        def fill(r):
            s = r // 32
            a = jnp.concatenate(pair(lane_in[m, s], lane_in[m, per + s]), axis=0)
            b = jnp.concatenate(pair(lane_in[m, 2 * per + s], lane_in[m, 3 * per + s]), axis=0)
            dif_fill(m, r, a, b, 1.0)

        over(n4, 32, fill)
        product(rhs.at[m], t_hi, t_lo, psi.at[m], n4)

    def measure_power(r):
        both = []
        for hi in range(2):
            p = jnp.zeros((64, 128), F32)
            for m in modes:
                z = psi[m, hi, pl.ds(r, 64), :]
                p = p + z * z
            both.append(p + swap(p))
        power[pl.ds(r, 64), :] = jnp.where(is_high(64), both[0], both[1]) * weight

    over(n4, 64, measure_power)

    for j in range(1, ring):
        to = (level + j) % ring
        pltpu.make_async_remote_copy(
            src_ref=power.at[pl.ds(pl.multiple_of(chunk * to, chunk), chunk)],
            dst_ref=sum_in.at[level],
            send_sem=sems.at[4],
            recv_sem=sems.at[5],
            device_id=at_level(to),
            device_id_type=MESH,
        ).start()

    @pl.when(own_band)
    def _():
        meas_in[rank % senders] = meas_out[here]
        drain(meas_in.at[pl.ds(0, senders - 1)], sems.at[3])

    @pl.when(jnp.logical_not(own_band))
    def _():
        drain(meas_in.at[pl.ds(0, senders)], sems.at[3])

    for t in range(senders):
        meas_own[4 * t : 4 * t + 4, :] = meas_in[t, 0:4, :]

    sum_in[level] = power[pl.ds(pl.multiple_of(chunk * level, chunk), chunk), :]
    drain(sum_in.at[pl.ds(0, ring - 1)], sems.at[5])
    total = sum_in[0]
    for j in range(1, ring):
        total = total + sum_in[j]
    ratio = meas_own[...] / jnp.sqrt(total + FLOOR_TERM) - 1.0
    ratio_own[...] = ratio
    for j in range(1, ring):
        to = (level + j) % ring
        pltpu.make_async_remote_copy(
            src_ref=ratio_own,
            dst_ref=ratio_all.at[level],
            send_sem=sems.at[6],
            recv_sem=sems.at[7],
            device_id=at_level(to),
            device_id_type=MESH,
        ).start()
    ratio_all[level] = ratio
    drain(ratio_all.at[pl.ds(0, ring - 1)], sems.at[7])

    for m in modes:

        def fill(r):
            f = ratio_all[r // chunk] * weight
            for hi, g in enumerate(halves(f, f)):
                put(rhs.at[m], n4, hi, r, psi[m, hi, pl.ds(r, chunk), :] * g, -1.0)

        over(n4, chunk, fill)
        product(rhs.at[m], t_hi, t_lo, prod.at[m], n4)

        def emit(r):
            s = r // 32
            z = [twiddle(prod[m, hi, pl.ds(r, 32), :], hi, r, -1.0) for hi in range(2)]
            for hi, b in enumerate(butterfly(z[0], z[1], -1.0)):
                first, second = pair(b[0:16], b[16:32])
                back_out[m, 2 * hi * per + s] = first
                back_out[m, (2 * hi + 1) * per + s] = second

        over(n4, 32, emit)

        for to in others:
            block_copy(m, back_out, back_in, back_sems, to)

    for m in modes:
        back_in[m, here] = back_out[m, here]
        drain(back_in.at[m, pl.ds(0, plane - 1)], back_sems.at[1, m])
        for hi in range(2):
            for t in range(tiles):
                v = [
                    trade([back_in[m, per * (2 * hi + lo) + 4 * t + d] for d in range(4)])
                    for lo in range(2)
                ]
                rows = [
                    v[lo][2 * part + qh] for part in range(2) for lo in range(2) for qh in range(2)
                ]
                put(rhs.at[m], n4, hi, 128 * t, jnp.concatenate(rows, axis=0).T, -1.0)
        product(rhs.at[m], t_hi, t_lo, prod.at[m], n4)
        stays = row_stays(128)
        for t in range(tiles):
            rows = slice(128 * t, 128 * t + 128)
            z = [twiddle(prod[m, hi, rows, :], hi, 128 * t, -1.0) for hi in range(2)]
            for hi, b in enumerate(butterfly(z[0], z[1], -1.0)):
                e = (w_re[hi, rows, :] * b - w_im[hi, rows, :] * swap(b)).T
                for part in range(2):
                    for lo in range(2):
                        cols = slice(128 * (2 * hi + lo), 128 * (2 * hi + lo) + 128)
                        got = e[64 * part + 32 * lo : 64 * part + 32 * lo + 32]
                        to_rows = slice(32 * part, 32 * part + 32)
                        upd[m, t, to_rows, cols] = jnp.where(stays, got, 0.0)
                        upd_out[m, t, to_rows, cols] = jnp.where(stays, 0.0, got)
            upd_copy[m][t].start()

    def finish(m, t, to_mode, with_kept, with_got):
        for part in range(2):
            source, target = (so_re, so_im)[part], (out_re, out_im)[part]
            to_rows = slice(32 * part, 32 * part + 32)
            for q in range(4):
                at = n4 * q + 128 * t
                col = lax.broadcasted_iota(jnp.int32, (32, 128), 1) + at
                left, right = slice(at, at + 128), slice(n + at, n + at + 128)
                low, high = source[to_mode, :, left], source[to_mode, :, right]
                for use, values, edge in (
                    (with_kept, upd, col_mine),
                    (with_got, upd_in, col_other),
                ):
                    if use:
                        v = values[m, t, to_rows, 128 * q : 128 * q + 128]
                        low = low + jnp.where(col < edge, 0.0, v)
                        high = high + jnp.where(col < edge, v, 0.0)
                target[to_mode, :, left] = low
                target[to_mode, :, right] = high

    if single:
        for t in range(tiles):
            finish(0, t, slot, True, False)
    for m in modes:
        for t in range(tiles):
            upd_copy[m][t].wait_recv()
            if single:
                finish(m, t, 1 - slot, False, True)
            else:
                finish(m, t, m, True, True)

    for m in modes:
        for t in range(tiles):
            win_copy[m][t].wait_send()
            upd_copy[m][t].wait_send()
        drain(lane_out.at[m, pl.ds(0, plane - 1)], lane_sems.at[0, m])
        drain(back_out.at[m, pl.ds(0, plane - 1)], back_sems.at[0, m])
    drain(pup_in.at[pl.ds(0, 2 * plane - 1)], sems.at[0])
    for mine_too in (True, False):

        @pl.when(gives & (own_band if mine_too else jnp.logical_not(own_band)))
        def _():
            drain(meas_out.at[pl.ds(0, plane - 1 if mine_too else plane)], sems.at[2])

    drain(sum_in.at[pl.ds(0, ring - 1)], sems.at[4])
    drain(ratio_all.at[pl.ds(0, ring - 1)], sems.at[6])


def body(groups, object_real, object_imag, pupil_real, pupil_imag, measured, source_mask, offsets):
    n = pupil_real.shape[1]
    plane = n // 32
    n4 = n // 4
    ring = 2 * groups
    consts = [jnp.asarray(t) for t in tables(n)]
    anyw = pl.BlockSpec(memory_space=pltpu.HBM)
    tiles = n4 // 128
    rows = pltpu.VMEM((2, tiles, 64, 512), F32)
    swaps = pltpu.SemaphoreType.DMA((2, 2 * tiles))
    blocks = pltpu.VMEM((2, plane, 16, 128), F32)
    quarters = pltpu.VMEM((2, n4, 128), F32)
    fields = pltpu.VMEM((2, 2, n4, 128), F32)
    chunks = pltpu.VMEM((ring, n4 // ring, 128), F32)
    like = lambda a: pltpu.VMEM(a.shape, a.dtype)
    pairs = pltpu.SemaphoreType.DMA((2, 2))
    scratch = [
        pltpu.SMEM(source_mask.shape, jnp.int32),
        pltpu.SMEM(offsets.T.shape, jnp.int32),
        *[like(a) for a in (object_real, object_imag, pupil_real, pupil_imag, measured)],
        *[like(a) for a in consts],
        rows,
        rows,
        pltpu.VMEM((2, plane, 8, 128), F32),
        pltpu.VMEM((2 * plane, 8, 128), F32),
        pltpu.VMEM((128, n // 8), F32),
        pltpu.VMEM((n // 8, 128), F32),
        pltpu.VMEM((plane, 8, 128), F32),
        pltpu.VMEM((n4 // ring // 4, 8, 128), F32),
        pltpu.VMEM((n4 // ring, 128), F32),
        pltpu.VMEM((2 * n, 128), F32),
        pltpu.VMEM((2 * n, 128), F32),
        quarters,
        quarters,
        pltpu.VMEM((2, n, 256), BF16),
        fields,
        blocks,
        blocks,
        fields,
        pltpu.VMEM((n4, 128), F32),
        chunks,
        pltpu.VMEM((n4 // ring, 128), F32),
        chunks,
        blocks,
        blocks,
        rows,
        rows,
        rows,
        pltpu.SemaphoreType.DMA((11,)),
        swaps,
        swaps,
        pairs,
        pairs,
        pltpu.SemaphoreType.DMA((9,)),
    ]
    def step(single):
        return pl.pallas_call(
            functools.partial(kernel, single, n, plane, groups),
            out_shape=[pltpu.VMEM(object_real.shape, F32)] * 2,
            in_specs=[anyw] * 11,
            out_specs=[pl.BlockSpec(memory_space=pltpu.VMEM)] * 2,
            scratch_shapes=scratch,
            compiler_params=pltpu.CompilerParams(
                collective_id=1 if single else 0, has_side_effects=True
            ),
            name="one_lit" if single else "two_lit",
        )

    operands = (
        object_real,
        object_imag,
        pupil_real,
        pupil_imag,
        measured,
        source_mask,
        offsets.T,
        *consts,
    )
    return lax.cond(jnp.sum(source_mask) > 1, step(False), step(True), *operands)


def solution(mesh):
    in_specs = (
        P("mode", "rows", None),
        P("mode", "rows", None),
        P("rows", None),
        P("rows", None),
        P(None, "rows", None),
        P(),
        P(),
    )
    out_specs = (P("mode", "rows", None), P("mode", "rows", None))
    return jax.shard_map(
        functools.partial(body, mesh.shape["mode"]),
        mesh=mesh,
        in_specs=in_specs,
        out_specs=out_specs,
        check_vma=False,
    )
```
